512 devices in a mesh: tm: 64 (over z, x), sx: 4 (over y), sy: 2 (over core).
Axes of the slice: x: 4, y: 4, z: 16, core: 2. Of those that a mesh axis runs over, the one named last changes fastest.
Arguments:
- sources: float32 [128, 32, 32, 128], P('tm', 'sx', 'sy'), may hold values from -6 to 6
- forward_states: float32 [128, 32, 32, 128], P('tm', 'sx', 'sy'), may hold values from -6 to 6
- terminal: float32 [32, 32, 128], P('sx', 'sy'), may hold values from -6 to 6
- damping: float32 [32, 32, 128], P('sx', 'sy'), may hold values from 0.001 to 0.1
- contact_stiff: float32 [8], replicated, may hold values from 0.001 to 1
- regions: int32 [128, 4, 4], P('tm', 'sx', 'sy'), may hold values from 0 to 7
Outputs:
- adjoint: float32 [128, 32, 32, 128], P('tm', 'sx', 'sy')
- damping_grad: float32 [32, 32, 128], P('sx', 'sy')
The draws below stay inside these ranges and needn't reach their ends.
Inputs may be any that keep to these rules, and one draw needn't show every extreme that they name: `regions`: region of a block of 8 x 8 columns of cells at a step.
All inputs are finite; a program needn't handle non-finite values.
Results may differ from the reference program's by a relative error of at most 0.0003.
Values sent between devices are 32-bit elements; how exact they have to be, the bound alone decides.
No kernel may reach another device: no remote copies, remote signals or barrier semaphores. Data moves between devices by JAX's collectives and lax.ppermute only.
A program may use at most 64 MiB of HBM per device.

```python
import math
import jax
import jax.numpy as jnp
import numpy as np
from jax import lax

CZ = 128
STEPS_DEV = 2
SWEEPS = 4
REGIONS = 8
BLOCK_CELLS = 8
NX = 32
NY = 32
NT = 128
N_TM = 64


def place_ends(result, stream_key, low, high):
    dims = result.shape
    place = [jax.random.randint(jax.random.fold_in(stream_key, axis), (), 0, dims[axis]) for axis in range(len(dims))]
    result = result.at[tuple(place)].set(low)
    longest = dims.index(max(dims))
    place[longest] = (place[longest] + 1) % dims[longest]
    return result.at[tuple(place)].set(high)


def block_scale(own_key, shape, shards, least, largest):
    def one(dim, parts):
        heights = jax.random.uniform(jax.random.fold_in(jax.random.fold_in(own_key, 6), dim), (parts,), jnp.float32, least / len(shards), largest / len(shards))
        return jnp.repeat(jnp.exp(heights), shape[dim] // parts).reshape((-1,) + (1,) * (len(shape) - dim - 1))

    level = one(*shards[0])
    for cut in shards[1:]:
        level = level * one(*cut)
    return level


def rank_bounds(number_of, lean):
    weights = [(1 << 20) // math.isqrt(rank ** lean) + 1 for rank in range(1, number_of + 1)]
    width = 1 + sum(weights) // (1 << 30)
    return np.cumsum(np.array([max(1, weight // width) for weight in weights]))


def skewed_ids(stream_key, shape, count, lean):
    table = rank_bounds(count, lean)
    ticket = jax.random.randint(jax.random.fold_in(stream_key, 1), shape, 0, int(table[count - 1]))
    standing = jnp.searchsorted(jnp.asarray(table, jnp.int32), ticket, side="right")
    return jax.random.permutation(jax.random.fold_in(stream_key, 2), count)[standing].astype(jnp.int32)


def gaussian(key, shape, scale, reach, shards=(), kind=jnp.bfloat16):
    values = scale * jax.random.normal(key, shape, jnp.float32)
    if shards:
        values = values * block_scale(key, shape, shards, -0.22, 0.18)
    return jnp.clip(values, -reach, reach).astype(kind)


def setup_inputs(seed: int = 0) -> dict:
    streams_of = jax.random.split(jax.random.key(seed), 7)
    sources = gaussian(streams_of[0], (NT, NX, NY, CZ), 1.0, 6.0, ((0, 64), (1, 4), (2, 2)), jnp.float32)
    forward_states = gaussian(streams_of[1], (NT, NX, NY, CZ), 1.0, 6.0, ((0, 64), (1, 4), (2, 2)), jnp.float32)
    terminal = gaussian(streams_of[2], (NX, NY, CZ), 1.0, 6.0, ((0, 4), (1, 2)), jnp.float32)
    damping = jnp.clip(jnp.exp(math.log(0.1) - 4.6051702 * jax.random.uniform(streams_of[3], (NX, NY, CZ), jnp.float32) ** block_scale(streams_of[3], (NX, NY, CZ), ((0, 4), (1, 2)), -0.2, 0.2)), 0.001, 0.1)
    contact_stiff = jnp.clip(jnp.exp(jax.random.uniform(streams_of[4], (REGIONS,), jnp.float32, math.log(0.001), math.log(1.0))), 0.001, 1.0)
    regions = place_ends(skewed_ids(streams_of[5], (NT, NX // BLOCK_CELLS, NY // BLOCK_CELLS), REGIONS, 2), jax.random.fold_in(streams_of[5], 3), 0, REGIONS - 1).astype(jnp.int32)
    return dict(sources=sources, forward_states=forward_states, terminal=terminal, damping=damping, contact_stiff=contact_stiff, regions=regions)


coupling = 0.5


def neighbours(field):
    padded = jnp.pad(field, 1)
    total = padded[2:, 1:-1, 1:-1] + padded[:-2, 1:-1, 1:-1]
    total = total + padded[1:-1, 2:, 1:-1] + padded[1:-1, :-2, 1:-1]
    total = total + padded[1:-1, 1:-1, 2:] + padded[1:-1, 1:-1, :-2]
    return total


def propagate(right, diagonal):
    field = right
    for sweep_index in range(SWEEPS):
        field = (right + coupling * neighbours(field)) / diagonal
    return field


def reaction(region_ids, contact_stiff, damping):
    labels = jnp.arange(REGIONS, dtype=jnp.int32)
    picked = jnp.sum(jnp.where(region_ids[:, :, None] == labels, contact_stiff, jnp.zeros_like(contact_stiff)), axis=2)
    spread = jnp.repeat(jnp.repeat(picked, BLOCK_CELLS, axis=0), BLOCK_CELLS, axis=1)
    return spread[:, :, None] + damping


def reference(sources, forward_states, terminal, damping, contact_stiff, regions):
    grid = damping.shape
    slab_src = sources.reshape((N_TM, STEPS_DEV) + grid)
    slab_states = forward_states.reshape((N_TM, STEPS_DEV) + grid)
    slab_reg = regions.reshape((N_TM, STEPS_DEV) + regions.shape[1:])
    slab_ids = jnp.arange(N_TM, dtype=jnp.int32)

    def first_pass(inputs):
        src_here, reg_here, slab_index = inputs
        field = jnp.where(slab_index == N_TM - 1, terminal, jnp.zeros_like(terminal))
        for position in range(STEPS_DEV - 1, -1, -1):
            diagonal = 1.0 + reaction(reg_here[position], contact_stiff, damping) + 6.0 * coupling
            field = propagate(field, diagonal) + src_here[position]
        return field

    coarse_rhs = lax.map(first_pass, (slab_src, slab_reg, slab_ids))

    def coarse_factor(region_first):
        return 1.0 / (1.0 + STEPS_DEV * reaction(region_first, contact_stiff, damping))

    factors = lax.map(coarse_factor, slab_reg[:, 0])

    def advance(carry, inputs):
        factor, rhs = inputs
        value = factor * carry + rhs
        return value, value

    final_carry, corrected = lax.scan(advance, jnp.zeros_like(terminal), (factors, coarse_rhs), reverse=True)
    incoming = jnp.concatenate([corrected[1:], terminal[None]], axis=0)

    def final_pass(inputs):
        src_here, reg_here, states_here, field, head = inputs
        layers = [head] + [head] * (STEPS_DEV - 1)
        for position in range(STEPS_DEV - 1, 0, -1):
            diagonal = 1.0 + reaction(reg_here[position], contact_stiff, damping) + 6.0 * coupling
            field = propagate(field, diagonal) + src_here[position]
            layers[position] = field
        stacked = jnp.stack(layers)
        return stacked, jnp.sum(stacked * states_here, axis=0)

    adjoint, partials = lax.map(final_pass, (slab_src, slab_reg, slab_states, incoming, corrected))
    damping_grad = -jnp.sum(partials, axis=0)
    return adjoint.reshape(sources.shape), damping_grad
```

```python
import functools
import jax
import jax.numpy as jnp
from jax import lax
from jax.experimental import pallas as pl
from jax.experimental.pallas import tpu as pltpu
from jax.sharding import PartitionSpec as P

F32 = jnp.float32
COUPLING = 0.5
CENTRE = 1.0 + 6.0 * COUPLING

NZ, NX4, ND = 16, 4, 8
X_GROUPS = [[z * NX4 + x for x in range(NX4)] for z in range(NZ)]
Z_GROUPS = [[z * NX4 + x for z in range(NZ)] for x in range(NX4)]

T_OWN = 16
SRC1 = (0, 32, 8)
DAMP = (32, 40, 12)
TERM = (72, 40, 12)
SRC0 = (112, 24, 4)
REACT = 136
ROWS1 = 144


def xy_neighbours(f):
    sub = lax.broadcasted_iota(jnp.int32, f.shape, 1)
    lane = lax.broadcasted_iota(jnp.int32, f.shape, 2)
    yl = lane % 16
    xp = pltpu.roll(f, 112, 2)
    xm = pltpu.roll(f, 16, 2)
    xpc = pltpu.roll(xp, 6, 1)
    xmc = pltpu.roll(xm, 2, 1)
    zero = jnp.zeros_like(f)
    total = jnp.where(lane < 112, xp, jnp.where(sub < 6, xpc, zero))
    total = total + jnp.where(lane >= 16, xm, jnp.where(sub >= 2, xmc, zero))
    yp = pltpu.roll(f, 127, 2)
    ym = pltpu.roll(f, 1, 2)
    even = (sub % 2) == 0
    ypc = pltpu.roll(pltpu.roll(f, 15, 2), 7, 1)
    ymc = pltpu.roll(pltpu.roll(f, 113, 2), 1, 1)
    total = total + jnp.where(yl < 15, yp, jnp.where(even, ypc, zero))
    total = total + jnp.where(yl > 0, ym, jnp.where(even, zero, ymc))
    return total


def phi(b, inv):
    n = b.shape[0]
    x = b
    for s in range(1, 5):
        nb = x[2:] + x[:-2] + xy_neighbours(x[1:-1])
        rows = slice(s, n - s)
        x = (b[rows] + COUPLING * nb) * inv[s - 1 : n - s - 1]
    return x


def row_mask(rows, halo, d):
    t = lax.broadcasted_iota(jnp.int32, (rows, 8, 128), 0) + d * T_OWN - halo
    return (t >= 0) & (t < 128)


def pack_kernel(stiff_ref, reg_ref, src_ref, damp_ref, term_ref, out_ref, pad):
    pad[...] = jnp.zeros_like(pad)

    def put(value, spec):
        off, rows, halo = spec
        pad[halo : halo + 128, :] = value.reshape(128, 128).T
        pad[halo + 128 : 2 * halo + 128, :] = jnp.zeros((halo, 128), F32)
        pad[0:halo, :] = jnp.zeros((halo, 128), F32)
        for d in range(ND):
            out_ref[d, off : off + rows, :] = pad[T_OWN * d : T_OWN * d + rows, :]

    put(src_ref[1], SRC1)
    put(damp_ref[...], DAMP)
    put(term_ref[...], TERM)
    put(src_ref[0], SRC0)
    yl = lax.broadcasted_iota(jnp.int32, (1, 128), 1) % 16
    rows = []
    for k in (1, 0):
        r0 = stiff_ref[reg_ref[2 * k]]
        r1 = stiff_ref[reg_ref[2 * k + 1]]
        rows.append(jnp.where(yl < 8, r0, r1).astype(F32))
    tail = jnp.concatenate(rows + [jnp.zeros((6, 128), F32)], axis=0)
    for d in range(ND):
        out_ref[d, REACT : REACT + 8, :] = tail


def spread(scr, recv_ref, off, rows, base=0):
    for s in range(ND):
        scr[pl.ds(s, rows, stride=8), :] = recv_ref[s, off : off + rows, :]
    return scr[0 : rows * 8, :].reshape(rows, 8, 128)


def first_kernel(idx_ref, recv_ref, out_ref, inv_ref, scr):
    d = idx_ref[2]
    last = (idx_ref[0] == NZ - 1) & (idx_ref[1] == NX4 - 1)
    react1 = recv_ref[:, REACT, :]
    react0 = recv_ref[:, REACT + 1, :]
    damp = spread(scr, recv_ref, DAMP[0], DAMP[1])
    inside = row_mask(40, 12, d)
    zero = jnp.zeros((40, 8, 128), F32)
    inv1 = jnp.where(inside, 1.0 / (CENTRE + (react1[None] + damp)), zero)
    inv0 = jnp.where(inside, 1.0 / (CENTRE + (react0[None] + damp)), zero)
    inv_ref[...] = inv1[9:31]
    term = spread(scr, recv_ref, TERM[0], TERM[1])
    term = jnp.where(last, term, zero)
    v = phi(term, inv1[1:39])
    v = v + spread(scr, recv_ref, SRC1[0], SRC1[1])
    rhs = phi(v, inv0[5:35])
    rhs = rhs + spread(scr, recv_ref, SRC0[0], SRC0[1])
    scr[0 : 24 * 8, :] = rhs.reshape(24 * 8, 128)
    for s in range(ND):
        q, sub = s // 2, s % 2
        out_ref[q, 24 * sub : 24 * sub + 24, :] = scr[pl.ds(s, 24, stride=8), :]
        out_ref[q, 48 + sub : 49 + sub, :] = recv_ref[s, REACT + 1 : REACT + 2, :]
    for q in range(NX4):
        out_ref[q, 50:56, :] = jnp.zeros((6, 128), F32)


def quarter_damp(idx_ref, recv_ref):
    x = idx_ref[1]
    rows = slice(DAMP[0] + 8, DAMP[0] + 32)
    return jnp.concatenate([recv_ref[2 * x, rows, :], recv_ref[2 * x + 1, rows, :]], axis=0)


def per_pair(r0, r1):
    return jnp.concatenate([jnp.broadcast_to(r0, (24, 128)), jnp.broadcast_to(r1, (24, 128))], axis=0)


def compose_kernel(idx_ref, recv1_ref, recv_ref, out_ref):
    damp = quarter_damp(idx_ref, recv1_ref)
    carry = recv_ref[3, 0:48, :]
    for x in (2, 1, 0):
        react = per_pair(recv_ref[x, 48:49, :], recv_ref[x, 49:50, :])
        carry = carry / (1.0 + 2.0 * (react + damp)) + recv_ref[x, 0:48, :]
    tail = jnp.concatenate([recv_ref[x, 48:50, :] for x in range(NX4)], axis=0)
    for z in range(NZ):
        out_ref[z, 0:48, :] = carry
        out_ref[z, 48:56, :] = tail


def scan_kernel(idx_ref, recv1_ref, recv2_ref, recv_ref, out_ref):
    z = idx_ref[0]
    damp = quarter_damp(idx_ref, recv1_ref)

    def step(i, carry):
        zz = NZ - 1 - i
        den = None
        for x in range(NX4):
            react = per_pair(recv_ref[zz, pl.ds(48 + 2 * x, 1), :], recv_ref[zz, pl.ds(49 + 2 * x, 1), :])
            term = 1.0 + 2.0 * (react + damp)
            den = term if den is None else den * term
        return carry / den + recv_ref[zz, 0:48, :]

    carry = lax.fori_loop(0, NZ - 1 - z, step, jnp.zeros((48, 128), F32))
    for x in (3, 2, 1, 0):
        react = per_pair(recv2_ref[x, 48:49, :], recv2_ref[x, 49:50, :])
        own = carry / (1.0 + 2.0 * (react + damp)) + recv2_ref[x, 0:48, :]
        out_ref[x, 0:48, :] = carry
        out_ref[x, 48:64, :] = own[4:20]
        out_ref[x, 64:80, :] = own[28:44]
        carry = own


def final_kernel(idx_ref, recv1_ref, inv_ref, recv_ref, out_ref, scr):
    last = (idx_ref[0] == NZ - 1) & (idx_ref[1] == NX4 - 1)
    for s in range(ND):
        q, sub = s // 2, s % 2
        incoming = recv_ref[q, 24 * sub : 24 * sub + 24, :]
        term = recv1_ref[s, TERM[0] + 8 : TERM[0] + 32, :]
        scr[pl.ds(s, 24, stride=8), :] = jnp.where(last, term, incoming)
        out_ref[s, 0:16, :] = recv_ref[q, 48 + 16 * sub : 64 + 16 * sub, :]
    w = phi(scr[...].reshape(24, 8, 128), inv_ref[...])
    scr[0:128, :] = w.reshape(128, 128)
    for s in range(ND):
        out_ref[s, 16:32, :] = scr[pl.ds(s, 16, stride=8), :] + recv1_ref[s, SRC1[0] + 8 : SRC1[0] + 24, :]


def unpack_kernel(recv_ref, state_ref, adj_ref, part_ref):
    total = None
    for k in range(2):
        rows = jnp.concatenate([recv_ref[s, 16 * k : 16 * k + 16, :] for s in range(ND)], axis=0)
        value = rows.T
        adj_ref[k] = value.reshape(8, 16, 128)
        prod = value * state_ref[k].reshape(128, 128)
        total = prod if total is None else total + prod
    part_ref[...] = (-total).reshape(4, 32, 128)


def sum_kernel(copies, recv_ref, out_ref):
    total = recv_ref[0]
    for i in range(1, recv_ref.shape[0]):
        total = total + recv_ref[i]
    for i in range(copies):
        out_ref[i] = total


VM = pl.BlockSpec(memory_space=pltpu.VMEM)
SM = pl.BlockSpec(memory_space=pltpu.SMEM)
INTERPRET = False


def call(kernel, outs, in_specs, scratch=(), name=None):
    shapes = [jax.ShapeDtypeStruct(s, F32) for s in outs]
    single = len(shapes) == 1
    return pl.pallas_call(
        kernel,
        out_shape=shapes[0] if single else shapes,
        in_specs=in_specs,
        out_specs=VM if single else [VM] * len(shapes),
        scratch_shapes=list(scratch),
        name=name,
        interpret=INTERPRET,
    )


def shards(sources, forward_states, terminal, damping, contact_stiff, regions):
    tm = lax.axis_index("tm")
    d = lax.axis_index("sx") * 2 + lax.axis_index("sy")
    idx = jnp.stack([tm // NX4, tm % NX4, d]).astype(jnp.int32)

    def over_space(v):
        return lax.all_to_all(v, ("sx", "sy"), 0, 0, tiled=True)

    def over_x(v):
        return lax.all_to_all(v, "tm", 0, 0, tiled=True, axis_index_groups=X_GROUPS)

    def over_z(v):
        return lax.all_to_all(v, "tm", 0, 0, tiled=True, axis_index_groups=Z_GROUPS)

    send1 = call(pack_kernel, [(ND, ROWS1, 128)], [SM, SM, VM, VM, VM], [pltpu.VMEM((152, 128), F32)], "pack")(
        contact_stiff, regions.reshape(4), sources, damping, terminal
    )
    recv1 = over_space(send1)
    send2, inv1 = call(first_kernel, [(NX4, 56, 128), (22, 8, 128)], [SM, VM], [pltpu.VMEM((320, 128), F32)], "first")(
        idx, recv1
    )
    recv2 = over_x(send2)
    sendz = call(compose_kernel, [(NZ, 56, 128)], [SM, VM, VM], name="compose")(idx, recv1, recv2)
    recvz = over_z(sendz)
    send3 = call(scan_kernel, [(NX4, 80, 128)], [SM, VM, VM, VM], name="scan")(idx, recv1, recv2, recvz)
    recv3 = over_x(send3)
    send4 = call(final_kernel, [(ND, 32, 128)], [SM, VM, VM, VM], [pltpu.VMEM((192, 128), F32)], "final")(
        idx, recv1, inv1, recv3
    )
    recv4 = over_space(send4)
    adjoint, part = call(unpack_kernel, [(2, 8, 16, 128), (4, 32, 128)], [VM, VM], name="unpack")(recv4, forward_states)
    part = over_x(part)
    part = call(functools.partial(sum_kernel, NZ), [(NZ, 32, 128)], [VM], name="sum_x")(part)
    part = over_z(part)
    part = call(functools.partial(sum_kernel, NX4), [(NX4, 32, 128)], [VM], name="sum_z")(part)
    grad = over_x(part)
    return adjoint, grad.reshape(8, 16, 128)


def solution(mesh):
    in_specs = (
        P("tm", "sx", "sy", None),
        P("tm", "sx", "sy", None),
        P("sx", "sy", None),
        P("sx", "sy", None),
        P(),
        P("tm", "sx", "sy"),
    )
    out_specs = (P("tm", "sx", "sy", None), P("sx", "sy", None))
    return jax.shard_map(shards, mesh=mesh, in_specs=in_specs, out_specs=out_specs, check_vma=False)
```

```python
import jax
import jax.numpy as jnp
from jax import lax
from jax.experimental import pallas as pl
from jax.experimental.pallas import tpu as pltpu
from jax.sharding import PartitionSpec as P

F32 = jnp.float32
COUPLING = 0.5
CENTRE = 1.0 + 6.0 * COUPLING

NZ, NX4, ND = 16, 4, 8

T_OWN = 16
SRC1 = (0, 32, 8)
DAMP = (32, 40, 12)
TERM = (72, 40, 12)
SRC0 = (112, 24, 4)
REACT = 136
ROWS1 = 144


def xy_neighbours(f):
    sub = lax.broadcasted_iota(jnp.int32, f.shape, 1)
    lane = lax.broadcasted_iota(jnp.int32, f.shape, 2)
    yl = lane % 16
    xp = pltpu.roll(f, 112, 2)
    xm = pltpu.roll(f, 16, 2)
    xpc = pltpu.roll(xp, 6, 1)
    xmc = pltpu.roll(xm, 2, 1)
    zero = jnp.zeros_like(f)
    total = jnp.where(lane < 112, xp, jnp.where(sub < 6, xpc, zero))
    total = total + jnp.where(lane >= 16, xm, jnp.where(sub >= 2, xmc, zero))
    yp = pltpu.roll(f, 127, 2)
    ym = pltpu.roll(f, 1, 2)
    even = (sub % 2) == 0
    ypc = pltpu.roll(pltpu.roll(f, 15, 2), 7, 1)
    ymc = pltpu.roll(pltpu.roll(f, 113, 2), 1, 1)
    total = total + jnp.where(yl < 15, yp, jnp.where(even, ypc, zero))
    total = total + jnp.where(yl > 0, ym, jnp.where(even, zero, ymc))
    return total


def phi(b, inv):
    n = b.shape[0]
    x = b
    for s in range(1, 5):
        nb = x[2:] + x[:-2] + xy_neighbours(x[1:-1])
        rows = slice(s, n - s)
        x = (b[rows] + COUPLING * nb) * inv[s - 1 : n - s - 1]
    return x


def row_mask(rows, halo, d):
    t = lax.broadcasted_iota(jnp.int32, (rows, 8, 128), 0) + d * T_OWN - halo
    return (t >= 0) & (t < 128)


def pack_kernel(stiff_ref, reg_ref, src_ref, damp_ref, term_ref, out_ref, pad):
    def put(value, spec):
        off, rows, halo = spec
        pad[halo : halo + 128, :] = value.reshape(128, 128).T
        pad[halo + 128 : 2 * halo + 128, :] = jnp.zeros((halo, 128), F32)
        pad[0:halo, :] = jnp.zeros((halo, 128), F32)
        for d in range(ND):
            out_ref[d, off : off + rows, :] = pad[T_OWN * d : T_OWN * d + rows, :]

    put(src_ref[1], SRC1)
    put(damp_ref[...], DAMP)
    put(term_ref[...], TERM)
    put(src_ref[0], SRC0)
    yl = lax.broadcasted_iota(jnp.int32, (8, 128), 1) % 16
    row = lax.broadcasted_iota(jnp.int32, (8, 128), 0)
    react = []
    for k in range(2):
        react.append(jnp.where(yl < 8, stiff_ref[reg_ref[k, 0, 0]], stiff_ref[reg_ref[k, 0, 1]]))
    tail = jnp.where(row == 0, react[1], react[0])
    for d in range(ND):
        out_ref[d, REACT : REACT + 8, :] = tail


def spread(scr, recv_ref, off, rows):
    for s in range(ND):
        scr[pl.ds(s, rows, stride=8), :] = recv_ref[s, off : off + rows, :]
    return scr[0 : rows * 8, :].reshape(rows, 8, 128)


def first_kernel(recv_ref, out_ref, inv_ref, rhs_ref, fac_ref, scr_d, scr_t, scr1, scr0):
    d = lax.axis_index("sx") * 2 + lax.axis_index("sy")
    last = lax.axis_index("tm") == NZ * NX4 - 1
    react1 = recv_ref[:, REACT, :]
    react0 = recv_ref[:, REACT + 1, :]
    damp = spread(scr_d, recv_ref, DAMP[0], DAMP[1])
    inside = row_mask(40, 12, d)
    zero = jnp.zeros((40, 8, 128), F32)
    inv1 = jnp.where(inside, 1.0 / (CENTRE + (react1[None] + damp)), zero)
    inv0 = jnp.where(inside, 1.0 / (CENTRE + (react0[None] + damp)), zero)
    inv_ref[...] = inv1[9:31]
    fac_ref[...] = 1.0 / (1.0 + 2.0 * (react0[None] + damp[12:28]))
    term = spread(scr_t, recv_ref, TERM[0], TERM[1])
    term = jnp.where(last, term, zero)
    v = phi(term, inv1[1:39])
    v = v + spread(scr1, recv_ref, SRC1[0], SRC1[1])
    rhs = phi(v, inv0[5:35])
    rhs = rhs + spread(scr0, recv_ref, SRC0[0], SRC0[1])
    rhs_ref[...] = rhs[4:20]
    scr_t[0 : 24 * 8, :] = rhs.reshape(24 * 8, 128)
    for s in range(ND):
        for i in range(3):
            out_ref[pl.ds(32 * s + i, 8, stride=4), :] = scr_t[pl.ds(64 * i + s, 8, stride=8), :]
        out_ref[pl.ds(32 * s + 3, 8, stride=4), :] = jnp.broadcast_to(recv_ref[s, REACT + 1 : REACT + 2, :], (8, 128))


def scan_kernel(recv1_ref, recv_ref, out_ref):
    t = lax.axis_index("tm")
    s, g = t // 8, t % 8
    sub = lax.broadcasted_iota(jnp.int32, (8, 128), 0)
    low = sub < 4
    damp = jnp.zeros((8, 128), F32)
    for i in range(3):
        row = recv1_ref[s, pl.ds(DAMP[0] + 8 + 8 * i + g, 1), :]
        damp = jnp.where(sub % 4 == i, row, damp)
    carry = jnp.zeros((8, 128), F32)
    for m in range(31, -1, -1):
        tile = recv_ref[8 * m : 8 * m + 8, :]
        react = jnp.where(low, tile[3:4], tile[7:8])
        fac = 1.0 / (1.0 + 2.0 * (react + damp))
        fac_hi = pltpu.roll(fac, 4, 0)
        rhs_hi = pltpu.roll(tile, 4, 0)
        next_lo = fac_hi * carry + rhs_hi
        out_ref[8 * m : 8 * m + 8, :] = jnp.where(low, next_lo, pltpu.roll(carry, 4, 0))
        carry = (fac * fac_hi) * carry + (fac * rhs_hi + tile)


def final_kernel(recv1_ref, inv_ref, rhs_ref, fac_ref, recv_ref, out_ref, scr):
    last = lax.axis_index("tm") == NZ * NX4 - 1
    for s in range(ND):
        for i in range(3):
            scr[pl.ds(64 * i + s, 8, stride=8), :] = recv_ref[pl.ds(32 * s + i, 8, stride=4), :]
    incoming = scr[...].reshape(24, 8, 128)
    own = fac_ref[...] * incoming[4:20] + rhs_ref[...]
    scr[0:128, :] = own.reshape(128, 128)
    for s in range(ND):
        out_ref[s, 0:16, :] = scr[pl.ds(s, 16, stride=8), :]
    for s in range(ND):
        scr[pl.ds(s, 24, stride=8), :] = recv1_ref[s, TERM[0] + 8 : TERM[0] + 32, :]
    w = phi(jnp.where(last, scr[...].reshape(24, 8, 128), incoming), inv_ref[...])
    scr[0:128, :] = w.reshape(128, 128)
    for s in range(ND):
        out_ref[s, 16:32, :] = scr[pl.ds(s, 16, stride=8), :] + recv1_ref[s, SRC1[0] + 8 : SRC1[0] + 24, :]


def unpack_kernel(recv_ref, state_ref, adj_ref, part_ref):
    total = None
    for k in range(2):
        rows = jnp.concatenate([recv_ref[s, 16 * k : 16 * k + 16, :] for s in range(ND)], axis=0)
        value = rows.T
        adj_ref[k] = value.reshape(8, 16, 128)
        prod = value * state_ref[k].reshape(128, 128)
        total = prod if total is None else total + prod
    part_ref[...] = -total


def sum_kernel(recv_ref, out_ref):
    total = recv_ref[0:8, :]
    for i in range(1, 16):
        total = total + recv_ref[8 * i : 8 * i + 8, :]
    total = total + pltpu.roll(total, 4, 0)
    total = total + pltpu.roll(total, 2, 0)
    for i in range(16):
        out_ref[8 * i : 8 * i + 8, :] = total


VM = pl.BlockSpec(memory_space=pltpu.VMEM)
SM = pl.BlockSpec(memory_space=pltpu.SMEM)
INTERPRET = False


def near(value):
    return pltpu.with_memory_space_constraint(value, pltpu.VMEM)


def call(kernel, outs, in_specs, scratch=(), name=None):
    shapes = [jax.ShapeDtypeStruct(s[1:], F32) if s[0] is None else pltpu.VMEM(s, F32) for s in outs]
    single = len(shapes) == 1
    return pl.pallas_call(
        kernel,
        out_shape=shapes[0] if single else shapes,
        in_specs=in_specs,
        out_specs=VM if single else [VM] * len(shapes),
        scratch_shapes=list(scratch),
        name=name,
        interpret=INTERPRET,
    )


def shards(sources, forward_states, terminal, damping, contact_stiff, regions):
    def over_space(v):
        return lax.all_to_all(v, ("sx", "sy"), 0, 0, tiled=True)

    def over_tm(v):
        slots = v.reshape(NZ * NX4, -1, 128)
        return lax.all_to_all(slots, "tm", 0, 0, tiled=True).reshape(v.shape)

    def scratch(rows):
        return pltpu.VMEM((rows, 128), F32)

    send1 = call(pack_kernel, [(ND, ROWS1, 128)], [SM, SM, VM, VM, VM], [scratch(152)], "pack")(
        contact_stiff, regions, sources, damping, terminal
    )
    recv1 = near(over_space(send1))
    send2, inv1, rhs, fac = call(
        first_kernel,
        [(256, 128), (22, 8, 128), (16, 8, 128), (16, 8, 128)],
        [VM],
        [scratch(320), scratch(320), scratch(256), scratch(192)],
        "first",
    )(recv1)
    inv1, rhs, fac = near(inv1), near(rhs), near(fac)
    recv2 = near(over_tm(send2))
    send3 = call(scan_kernel, [(256, 128)], [VM, VM], name="scan")(recv1, recv2)
    recv3 = near(over_tm(send3))
    send4 = call(final_kernel, [(ND, 32, 128)], [VM] * 5, [scratch(192)], "final")(
        recv1, inv1, rhs, fac, recv3
    )
    recv4 = near(over_space(send4))
    adjoint, part = call(unpack_kernel, [(None, 2, 8, 16, 128), (128, 128)], [VM, VM], name="unpack")(
        recv4, forward_states
    )
    part = near(over_tm(part))
    part = call(sum_kernel, [(128, 128)], [VM], name="sum")(part)
    grad = over_tm(part)
    return adjoint, grad.reshape(8, 16, 128)


def solution(mesh):
    in_specs = (
        P("tm", "sx", "sy", None),
        P("tm", "sx", "sy", None),
        P("sx", "sy", None),
        P("sx", "sy", None),
        P(),
        P("tm", "sx", "sy"),
    )
    out_specs = (P("tm", "sx", "sy", None), P("sx", "sy", None))
    return jax.shard_map(shards, mesh=mesh, in_specs=in_specs, out_specs=out_specs, check_vma=False)
```

```python
import jax
import jax.numpy as jnp
from jax import lax
from jax.experimental import pallas as pl
from jax.experimental.pallas import tpu as pltpu
from jax.sharding import Mesh
from jax.sharding import PartitionSpec as P

F32 = jnp.float32
COUPLING = 0.5
CENTRE = 1.0 + 6.0 * COUPLING

NZ, NX4, ND = 16, 4, 8

T_OWN = 16
SRC1 = (0, 32, 8)
DAMP = (32, 40, 12)
TERM = (72, 40, 12)
SRC0 = (112, 24, 4)
ST0 = (136, 16, 0)
ST1 = (152, 16, 0)
REACT = 168
ROWS1 = 176


def xy_neighbours(f):
    sub = lax.broadcasted_iota(jnp.int32, f.shape, 1)
    lane = lax.broadcasted_iota(jnp.int32, f.shape, 2)
    yl = lane % 16
    xp = pltpu.roll(f, 112, 2)
    xm = pltpu.roll(f, 16, 2)
    xpc = pltpu.roll(xp, 6, 1)
    xmc = pltpu.roll(xm, 2, 1)
    zero = jnp.zeros_like(f)
    total = jnp.where(lane < 112, xp, jnp.where(sub < 6, xpc, zero))
    total = total + jnp.where(lane >= 16, xm, jnp.where(sub >= 2, xmc, zero))
    yp = pltpu.roll(f, 127, 2)
    ym = pltpu.roll(f, 1, 2)
    even = (sub % 2) == 0
    ypc = pltpu.roll(pltpu.roll(f, 15, 2), 7, 1)
    ymc = pltpu.roll(pltpu.roll(f, 113, 2), 1, 1)
    total = total + jnp.where(yl < 15, yp, jnp.where(even, ypc, zero))
    total = total + jnp.where(yl > 0, ym, jnp.where(even, zero, ymc))
    return total


def phi(b, inv):
    n = b.shape[0]
    x = b
    for s in range(1, 5):
        nb = x[2:] + x[:-2] + xy_neighbours(x[1:-1])
        rows = slice(s, n - s)
        x = (b[rows] + COUPLING * nb) * inv[s - 1 : n - s - 1]
    return x


def row_mask(rows, halo, d):
    t = lax.broadcasted_iota(jnp.int32, (rows, 8, 128), 0) + d * T_OWN - halo
    return (t >= 0) & (t < 128)


def slab():
    return lax.axis_index("tz") * NX4 + lax.axis_index("tx")


def space():
    return lax.axis_index("sx") * 2 + lax.axis_index("sy")


def pack_kernel(stiff_ref, reg_ref, src_ref, damp_ref, term_ref, state_ref, out_ref, pad):
    def put(value, spec):
        off, rows, halo = spec
        pad[halo : halo + 128, :] = value.reshape(128, 128).T
        if halo:
            pad[halo + 128 : 2 * halo + 128, :] = jnp.zeros((halo, 128), F32)
            pad[0:halo, :] = jnp.zeros((halo, 128), F32)
        for d in range(ND):
            out_ref[d, off : off + rows, :] = pad[T_OWN * d : T_OWN * d + rows, :]

    put(src_ref[1], SRC1)
    put(damp_ref[...], DAMP)
    put(term_ref[...], TERM)
    put(src_ref[0], SRC0)
    put(state_ref[0], ST0)
    put(state_ref[1], ST1)
    yl = lax.broadcasted_iota(jnp.int32, (8, 128), 1) % 16
    row = lax.broadcasted_iota(jnp.int32, (8, 128), 0)
    react = []
    for k in range(2):
        react.append(jnp.where(yl < 8, stiff_ref[reg_ref[k, 0, 0]], stiff_ref[reg_ref[k, 0, 1]]))
    tail = jnp.where(row == 0, react[1], react[0])
    for d in range(ND):
        out_ref[d, REACT : REACT + 8, :] = tail


def spread(scr, recv_ref, off, rows):
    for s in range(ND):
        scr[pl.ds(s, rows, stride=8), :] = recv_ref[s, off : off + rows, :]
    return scr[0 : rows * 8, :].reshape(rows, 8, 128)


def first_kernel(recv_ref, out_ref, inv_ref, rhs_ref, fac_ref, scr_d, scr_t, scr1, scr0):
    d = space()
    last = slab() == NZ * NX4 - 1
    react1 = recv_ref[:, REACT, :]
    react0 = recv_ref[:, REACT + 1, :]
    damp = spread(scr_d, recv_ref, DAMP[0], DAMP[1])
    inside = row_mask(40, 12, d)
    zero = jnp.zeros((40, 8, 128), F32)
    inv1 = jnp.where(inside, 1.0 / (CENTRE + (react1[None] + damp)), zero)
    inv0 = jnp.where(inside, 1.0 / (CENTRE + (react0[None] + damp)), zero)
    inv_ref[...] = inv1[9:31]
    fac_ref[...] = 1.0 / (1.0 + 2.0 * (react0[None] + damp[12:28]))
    term = spread(scr_t, recv_ref, TERM[0], TERM[1])
    term = jnp.where(last, term, zero)
    v = phi(term, inv1[1:39])
    v = v + spread(scr1, recv_ref, SRC1[0], SRC1[1])
    rhs = phi(v, inv0[5:35])
    rhs = rhs + spread(scr0, recv_ref, SRC0[0], SRC0[1])
    rhs_ref[...] = rhs[4:20]
    scr_t[0 : 24 * 8, :] = rhs.reshape(24 * 8, 128)
    for s in range(ND):
        for i in range(3):
            out_ref[pl.ds(32 * s + i, 8, stride=4), :] = scr_t[pl.ds(64 * i + s, 8, stride=8), :]
        out_ref[pl.ds(32 * s + 3, 8, stride=4), :] = jnp.broadcast_to(recv_ref[s, REACT + 1 : REACT + 2, :], (8, 128))


def scan_kernel(recv1_ref, recv_ref, out_ref):
    t = slab()
    s, g = t // 8, t % 8
    sub = lax.broadcasted_iota(jnp.int32, (8, 128), 0)
    low = sub < 4
    damp = jnp.zeros((8, 128), F32)
    for i in range(3):
        row = recv1_ref[s, pl.ds(DAMP[0] + 8 + 8 * i + g, 1), :]
        damp = jnp.where(sub % 4 == i, row, damp)
    carry = jnp.zeros((8, 128), F32)
    for m in range(31, -1, -1):
        tile = recv_ref[8 * m : 8 * m + 8, :]
        react = jnp.where(low, tile[3:4], tile[7:8])
        fac = 1.0 / (1.0 + 2.0 * (react + damp))
        fac_hi = pltpu.roll(fac, 4, 0)
        rhs_hi = pltpu.roll(tile, 4, 0)
        next_lo = fac_hi * carry + rhs_hi
        out_ref[8 * m : 8 * m + 8, :] = jnp.where(low, next_lo, pltpu.roll(carry, 4, 0))
        carry = (fac * fac_hi) * carry + (fac * rhs_hi + tile)


def final_kernel(recv1_ref, inv_ref, rhs_ref, fac_ref, recv_ref, adj_ref, part_ref, scr, scr_o):
    last = slab() == NZ * NX4 - 1
    for s in range(ND):
        for i in range(3):
            scr[pl.ds(64 * i + s, 8, stride=8), :] = recv_ref[pl.ds(32 * s + i, 8, stride=4), :]
    incoming = scr[...].reshape(24, 8, 128)
    own = fac_ref[...] * incoming[4:20] + rhs_ref[...]
    scr_o[...] = own.reshape(128, 128)
    for s in range(ND):
        scr[pl.ds(s, 24, stride=8), :] = recv1_ref[s, TERM[0] + 8 : TERM[0] + 32, :]
    w = phi(jnp.where(last, scr[...].reshape(24, 8, 128), incoming), inv_ref[...])
    scr[0:128, :] = w.reshape(128, 128)
    for s in range(ND):
        adj0 = scr_o[pl.ds(s, 16, stride=8), :]
        adj1 = scr[pl.ds(s, 16, stride=8), :] + recv1_ref[s, SRC1[0] + 8 : SRC1[0] + 24, :]
        adj_ref[s, 0:16, :] = adj0
        adj_ref[s, 16:32, :] = adj1
        part = -(adj0 * recv1_ref[s, ST0[0] : ST0[0] + 16, :] + adj1 * recv1_ref[s, ST1[0] : ST1[0] + 16, :])
        for x in range(NX4):
            row = (x * ND + s) * 4
            part_ref[row : row + 4, :] = part[4 * x : 4 * x + 4]


def unpack_kernel(recv_ref, adj_ref, buf, sem):
    copy = pltpu.make_async_copy(recv_ref.at[:, space()], buf, sem)
    copy.start()
    copy.wait()
    for k in range(2):
        rows = jnp.concatenate([buf[s, 16 * k : 16 * k + 16, :] for s in range(ND)], axis=0)
        adj_ref[k] = rows.T.reshape(8, 16, 128)


def sum_kernel(recv_ref, out_ref):
    total = recv_ref[0:32, :]
    for i in range(1, recv_ref.shape[0] // 32):
        total = total + recv_ref[32 * i : 32 * i + 32, :]
    for i in range(out_ref.shape[0] // 32):
        out_ref[32 * i : 32 * i + 32, :] = total


def grad_kernel(recv_ref, out_ref, scr):
    for x in range(NX4):
        for d in range(ND):
            scr[16 * d + 4 * x : 16 * d + 4 * x + 4, :] = recv_ref[32 * x + 4 * d : 32 * x + 4 * d + 4, :]
    out_ref[...] = scr[...].T.reshape(8, 16, 128)


VM = pl.BlockSpec(memory_space=pltpu.VMEM)
SM = pl.BlockSpec(memory_space=pltpu.SMEM)
INTERPRET = False


def near(value):
    return pltpu.with_memory_space_constraint(value, pltpu.VMEM)


def call(kernel, outs, in_specs, scratch=(), name=None):
    shapes = [jax.ShapeDtypeStruct(s[1:], F32) if s[0] is None else pltpu.VMEM(s, F32) for s in outs]
    single = len(shapes) == 1
    return pl.pallas_call(
        kernel,
        out_shape=shapes[0] if single else shapes,
        in_specs=in_specs,
        out_specs=VM if single else [VM] * len(shapes),
        scratch_shapes=list(scratch),
        name=name,
        interpret=INTERPRET,
    )


def shards(sources, forward_states, terminal, damping, contact_stiff, regions):
    def exchange(v, axes):
        count = 1
        for axis in axes:
            count *= lax.axis_size(axis)
        slots = v.reshape(count, -1, 128)
        return near(lax.all_to_all(slots, axes, 0, 0, tiled=True).reshape(v.shape))

    tm, xy, plane = ("tz", "tx"), ("sx", "sy"), ("tx", "sx", "sy")

    def scratch(rows):
        return pltpu.VMEM((rows, 128), F32)

    send1 = call(pack_kernel, [(ND, ROWS1, 128)], [SM, SM, VM, VM, VM, VM], [scratch(152)], "pack")(
        contact_stiff, regions, sources, damping, terminal, forward_states
    )
    recv1 = exchange(send1, xy)
    send2, inv1, rhs, fac = call(
        first_kernel,
        [(256, 128), (22, 8, 128), (16, 8, 128), (16, 8, 128)],
        [VM],
        [scratch(320), scratch(320), scratch(256), scratch(192)],
        "first",
    )(recv1)
    inv1, rhs, fac = near(inv1), near(rhs), near(fac)
    recv2 = exchange(send2, tm)
    send3 = call(scan_kernel, [(256, 128)], [VM, VM], name="scan")(recv1, recv2)
    recv3 = exchange(send3, tm)
    layers, part = call(
        final_kernel, [(None, ND, 32, 128), (128, 128)], [VM] * 5, [scratch(192), scratch(128)], "final"
    )(recv1, inv1, rhs, fac, recv3)
    layers = lax.all_gather(layers, xy, axis=0, tiled=False)
    adjoint = call(
        unpack_kernel,
        [(None, 2, 8, 16, 128)],
        [pl.BlockSpec(memory_space=pl.ANY)],
        [pltpu.VMEM((ND, 32, 128), F32), pltpu.SemaphoreType.DMA],
        "unpack",
    )(layers)
    part = call(sum_kernel, [(512, 128)], [VM], name="sum_x")(exchange(part, plane))
    part = call(sum_kernel, [(128, 128)], [VM], name="sum_z")(exchange(part, ("tz",)))
    grad = call(grad_kernel, [(None, 8, 16, 128)], [VM], [scratch(128)], "grad")(exchange(part, ("tx",)))
    return adjoint, grad


def solution(mesh):
    split = Mesh(mesh.devices.reshape(NZ, NX4, 4, 2), ("tz", "tx", "sx", "sy"))
    tm = ("tz", "tx")
    in_specs = (
        P(tm, "sx", "sy", None),
        P(tm, "sx", "sy", None),
        P("sx", "sy", None),
        P("sx", "sy", None),
        P(),
        P(tm, "sx", "sy"),
    )
    out_specs = (P(tm, "sx", "sy", None), P("sx", "sy", None))
    return jax.shard_map(shards, mesh=split, in_specs=in_specs, out_specs=out_specs, check_vma=False)
```

```python
import jax
import jax.numpy as jnp
from jax import lax
from jax.experimental import pallas as pl
from jax.experimental.pallas import tpu as pltpu
from jax.sharding import Mesh
from jax.sharding import PartitionSpec as P

F32 = jnp.float32
COUPLING = 0.5
CENTRE = 1.0 + 6.0 * COUPLING

NH, NL, ND = 8, 8, 8

T_OWN = 16
SRC1 = (0, 32, 8)
DAMP = (32, 40, 12)
TERM = (72, 40, 12)
SRC0 = (112, 24, 4)
REACT = 136
ROWS1 = 144


def xy_neighbours(f):
    sub = lax.broadcasted_iota(jnp.int32, f.shape, 1)
    lane = lax.broadcasted_iota(jnp.int32, f.shape, 2)
    yl = lane % 16
    xp = pltpu.roll(f, 112, 2)
    xm = pltpu.roll(f, 16, 2)
    xpc = pltpu.roll(xp, 6, 1)
    xmc = pltpu.roll(xm, 2, 1)
    zero = jnp.zeros_like(f)
    total = jnp.where(lane < 112, xp, jnp.where(sub < 6, xpc, zero))
    total = total + jnp.where(lane >= 16, xm, jnp.where(sub >= 2, xmc, zero))
    yp = pltpu.roll(f, 127, 2)
    ym = pltpu.roll(f, 1, 2)
    even = (sub % 2) == 0
    ypc = pltpu.roll(pltpu.roll(f, 15, 2), 7, 1)
    ymc = pltpu.roll(pltpu.roll(f, 113, 2), 1, 1)
    total = total + jnp.where(yl < 15, yp, jnp.where(even, ypc, zero))
    total = total + jnp.where(yl > 0, ym, jnp.where(even, zero, ymc))
    return total


def phi(b, inv):
    n = b.shape[0]
    x = b
    for s in range(1, 5):
        nb = x[2:] + x[:-2] + xy_neighbours(x[1:-1])
        rows = slice(s, n - s)
        x = (b[rows] + COUPLING * nb) * inv[s - 1 : n - s - 1]
    return x


def row_mask(rows, halo, d):
    t = lax.broadcasted_iota(jnp.int32, (rows, 8, 128), 0) + d * T_OWN - halo
    return (t >= 0) & (t < 128)


def is_last_slab():
    return (lax.axis_index("th") == NH - 1) & (lax.axis_index("tl") == NL - 1)


def pack_kernel(stiff_ref, reg_ref, src_ref, damp_ref, term_ref, out_ref, pad):
    def put(value, spec):
        off, rows, halo = spec
        pad[halo : halo + 128, :] = value.reshape(128, 128).T
        pad[halo + 128 : 2 * halo + 128, :] = jnp.zeros((halo, 128), F32)
        pad[0:halo, :] = jnp.zeros((halo, 128), F32)
        for d in range(ND):
            out_ref[d, off : off + rows, :] = pad[T_OWN * d : T_OWN * d + rows, :]

    put(src_ref[1], SRC1)
    put(damp_ref[...], DAMP)
    put(term_ref[...], TERM)
    put(src_ref[0], SRC0)
    yl = lax.broadcasted_iota(jnp.int32, (8, 128), 1) % 16
    row = lax.broadcasted_iota(jnp.int32, (8, 128), 0)
    react = []
    for k in range(2):
        react.append(jnp.where(yl < 8, stiff_ref[reg_ref[k, 0, 0]], stiff_ref[reg_ref[k, 0, 1]]))
    tail = jnp.where(row == 0, react[1], react[0])
    for d in range(ND):
        out_ref[d, REACT : REACT + 8, :] = tail


def spread(scr, recv_ref, off, rows):
    for s in range(ND):
        scr[pl.ds(s, rows, stride=8), :] = recv_ref[s, off : off + rows, :]
    return scr[0 : rows * 8, :].reshape(rows, 8, 128)


def first_kernel(recv_ref, out_ref, inv_ref, rhs_ref, fac_ref, scr_d, scr_t, scr1, scr0):
    d = lax.axis_index("sx") * 2 + lax.axis_index("sy")
    last = is_last_slab()
    react1 = recv_ref[:, REACT, :]
    react0 = recv_ref[:, REACT + 1, :]
    damp = spread(scr_d, recv_ref, DAMP[0], DAMP[1])
    inside = row_mask(40, 12, d)
    zero = jnp.zeros((40, 8, 128), F32)
    inv1 = jnp.where(inside, 1.0 / (CENTRE + (react1[None] + damp)), zero)
    inv0 = jnp.where(inside, 1.0 / (CENTRE + (react0[None] + damp)), zero)
    inv_ref[...] = inv1[9:31]
    fac_ref[...] = 1.0 / (1.0 + 2.0 * (react0[None] + damp[12:28]))
    term = spread(scr_t, recv_ref, TERM[0], TERM[1])
    term = jnp.where(last, term, zero)
    v = phi(term, inv1[1:39])
    v = v + spread(scr1, recv_ref, SRC1[0], SRC1[1])
    rhs = phi(v, inv0[5:35])
    rhs = rhs + spread(scr0, recv_ref, SRC0[0], SRC0[1])
    rhs_ref[...] = rhs[4:20]
    scr_t[0 : 24 * 8, :] = rhs.reshape(24 * 8, 128)
    for s in range(ND):
        out_ref[32 * s : 32 * s + 24, :] = scr_t[pl.ds(s, 24, stride=8), :]
        out_ref[32 * s + 24 : 32 * s + 32, :] = jnp.broadcast_to(recv_ref[s, REACT + 1 : REACT + 2, :], (8, 128))


def own_damp(recv1_ref):
    return recv1_ref[lax.axis_index("tl"), DAMP[0] + 8 : DAMP[0] + 32, :]


def compose_kernel(recv1_ref, recv_ref, out_ref):
    damp = own_damp(recv1_ref)
    carry = recv_ref[32 * (NL - 1) : 32 * (NL - 1) + 24, :]
    for j in range(NL - 2, -1, -1):
        react = recv_ref[32 * j + 24 : 32 * j + 25, :]
        carry = carry / (1.0 + 2.0 * (react + damp)) + recv_ref[32 * j : 32 * j + 24, :]
    tail = jnp.concatenate([recv_ref[32 * j + 24 : 32 * j + 25, :] for j in range(NL)], axis=0)
    for h in range(NH):
        out_ref[32 * h : 32 * h + 24, :] = carry
        out_ref[32 * h + 24 : 32 * h + 32, :] = tail


def scan_kernel(recv1_ref, recv2_ref, recv_ref, out_ref):
    me = lax.axis_index("th")
    damp = own_damp(recv1_ref)
    carry = jnp.zeros((24, 128), F32)
    for h in range(NH - 1, 0, -1):
        den = None
        for j in range(NL):
            term = 1.0 + 2.0 * (recv_ref[32 * h + 24 + j : 32 * h + 25 + j, :] + damp)
            den = term if den is None else den * term
        carry = jnp.where(h > me, carry / den + recv_ref[32 * h : 32 * h + 24, :], carry)
    for j in range(NL - 1, -1, -1):
        out_ref[24 * j : 24 * j + 24, :] = carry
        react = recv2_ref[32 * j + 24 : 32 * j + 25, :]
        carry = carry / (1.0 + 2.0 * (react + damp)) + recv2_ref[32 * j : 32 * j + 24, :]


def final_kernel(recv1_ref, inv_ref, rhs_ref, fac_ref, recv_ref, out_ref, scr):
    last = is_last_slab()
    for s in range(ND):
        scr[pl.ds(s, 24, stride=8), :] = recv_ref[24 * s : 24 * s + 24, :]
    incoming = scr[...].reshape(24, 8, 128)
    own = fac_ref[...] * incoming[4:20] + rhs_ref[...]
    scr[0:128, :] = own.reshape(128, 128)
    for s in range(ND):
        out_ref[s, 0:16, :] = scr[pl.ds(s, 16, stride=8), :]
    for s in range(ND):
        scr[pl.ds(s, 24, stride=8), :] = recv1_ref[s, TERM[0] + 8 : TERM[0] + 32, :]
    w = phi(jnp.where(last, scr[...].reshape(24, 8, 128), incoming), inv_ref[...])
    scr[0:128, :] = w.reshape(128, 128)
    for s in range(ND):
        out_ref[s, 16:32, :] = scr[pl.ds(s, 16, stride=8), :] + recv1_ref[s, SRC1[0] + 8 : SRC1[0] + 24, :]


def unpack_kernel(recv_ref, state_ref, adj_ref, part_ref):
    total = None
    for k in range(2):
        rows = jnp.concatenate([recv_ref[s, 16 * k : 16 * k + 16, :] for s in range(ND)], axis=0)
        value = rows.T
        adj_ref[k] = value.reshape(8, 16, 128)
        prod = value * state_ref[k].reshape(128, 128)
        total = prod if total is None else total + prod
    part_ref[...] = -total


def sum_kernel(recv_ref, out_ref):
    total = recv_ref[0:16, :]
    for i in range(1, 8):
        total = total + recv_ref[16 * i : 16 * i + 16, :]
    for i in range(8):
        out_ref[16 * i : 16 * i + 16, :] = total


VM = pl.BlockSpec(memory_space=pltpu.VMEM)
SM = pl.BlockSpec(memory_space=pltpu.SMEM)
INTERPRET = False


def near(value):
    return pltpu.with_memory_space_constraint(value, pltpu.VMEM)


def call(kernel, outs, in_specs, scratch=(), name=None):
    shapes = [jax.ShapeDtypeStruct(s[1:], F32) if s[0] is None else pltpu.VMEM(s, F32) for s in outs]
    single = len(shapes) == 1
    return pl.pallas_call(
        kernel,
        out_shape=shapes[0] if single else shapes,
        in_specs=in_specs,
        out_specs=VM if single else [VM] * len(shapes),
        scratch_shapes=list(scratch),
        name=name,
        interpret=INTERPRET,
    )


def shards(sources, forward_states, terminal, damping, contact_stiff, regions):
    def exchange(v, axes):
        slots = v.reshape(8, -1, 128)
        return lax.all_to_all(slots, axes, 0, 0, tiled=True).reshape(v.shape)

    def scratch(rows):
        return pltpu.VMEM((rows, 128), F32)

    send1 = call(pack_kernel, [(ND, ROWS1, 128)], [SM, SM, VM, VM, VM], [scratch(152)], "pack")(
        contact_stiff, regions, sources, damping, terminal
    )
    recv1 = near(exchange(send1, ("sx", "sy")))
    send2, inv1, rhs, fac = call(
        first_kernel,
        [(256, 128), (22, 8, 128), (16, 8, 128), (16, 8, 128)],
        [VM],
        [scratch(320), scratch(320), scratch(256), scratch(192)],
        "first",
    )(recv1)
    inv1, rhs, fac = near(inv1), near(rhs), near(fac)
    recv2 = near(exchange(send2, "tl"))
    send_h = call(compose_kernel, [(256, 128)], [VM, VM], name="compose")(recv1, recv2)
    recv_h = near(exchange(send_h, "th"))
    send3 = call(scan_kernel, [(192, 128)], [VM] * 3, name="scan")(recv1, recv2, recv_h)
    recv3 = near(exchange(send3, "tl"))
    send4 = call(final_kernel, [(ND, 32, 128)], [VM] * 5, [scratch(192)], "final")(recv1, inv1, rhs, fac, recv3)
    recv4 = near(exchange(send4, ("sx", "sy")))
    adjoint, part = call(unpack_kernel, [(None, 2, 8, 16, 128), (128, 128)], [VM, VM], name="unpack")(
        recv4, near(forward_states)
    )
    for axis in ("tl", "th"):
        part = call(sum_kernel, [(128, 128)], [VM], name="sum_" + axis)(near(exchange(part, axis)))
    grad = exchange(part, "tl")
    return adjoint, grad.reshape(8, 16, 128)


def solution(mesh):
    split = Mesh(mesh.devices.reshape(NH, NL, 4, 2), ("th", "tl", "sx", "sy"))
    tm = ("th", "tl")
    in_specs = (
        P(tm, "sx", "sy", None),
        P(tm, "sx", "sy", None),
        P("sx", "sy", None),
        P("sx", "sy", None),
        P(),
        P(tm, "sx", "sy"),
    )
    out_specs = (P(tm, "sx", "sy", None), P("sx", "sy", None))
    return jax.shard_map(shards, mesh=split, in_specs=in_specs, out_specs=out_specs, check_vma=False)
```

```python
import jax
import jax.numpy as jnp
from jax import lax
from jax.experimental import pallas as pl
from jax.experimental.pallas import tpu as pltpu
from jax.sharding import Mesh
from jax.sharding import PartitionSpec as P

F32 = jnp.float32
COUPLING = 0.5
CENTRE = 1.0 + 6.0 * COUPLING

NH, NL, ND = 8, 8, 8

T_OWN = 16
SRC1 = (0, 32, 8)
DAMP = (32, 40, 12)
TERM = (72, 40, 12)
SRC0 = (112, 24, 4)
REACT = 136
ROWS1 = 144


def xy_neighbours(f):
    sub = lax.broadcasted_iota(jnp.int32, f.shape, 1)
    lane = lax.broadcasted_iota(jnp.int32, f.shape, 2)
    yl = lane % 16
    xp = pltpu.roll(f, 112, 2)
    xm = pltpu.roll(f, 16, 2)
    xpc = pltpu.roll(xp, 6, 1)
    xmc = pltpu.roll(xm, 2, 1)
    zero = jnp.zeros_like(f)
    total = jnp.where(lane < 112, xp, jnp.where(sub < 6, xpc, zero))
    total = total + jnp.where(lane >= 16, xm, jnp.where(sub >= 2, xmc, zero))
    yp = pltpu.roll(f, 127, 2)
    ym = pltpu.roll(f, 1, 2)
    even = (sub % 2) == 0
    ypc = pltpu.roll(pltpu.roll(f, 15, 2), 7, 1)
    ymc = pltpu.roll(pltpu.roll(f, 113, 2), 1, 1)
    total = total + jnp.where(yl < 15, yp, jnp.where(even, ypc, zero))
    total = total + jnp.where(yl > 0, ym, jnp.where(even, zero, ymc))
    return total


def phi(b, inv):
    n = b.shape[0]
    x = b
    for s in range(1, 5):
        nb = x[2:] + x[:-2] + xy_neighbours(x[1:-1])
        rows = slice(s, n - s)
        x = (b[rows] + COUPLING * nb) * inv[s - 1 : n - s - 1]
    return x


def row_mask(rows, halo, d):
    t = lax.broadcasted_iota(jnp.int32, (rows, 8, 128), 0) + d * T_OWN - halo
    return (t >= 0) & (t < 128)


def is_last_slab():
    return (lax.axis_index("th") == NH - 1) & (lax.axis_index("tl") == NL - 1)


def space():
    return lax.axis_index("sx") * 2 + lax.axis_index("sy")


def pack_kernel(stiff_ref, reg_ref, src_ref, damp_ref, term_ref, out_ref, pad):
    def put(value, spec):
        off, rows, halo = spec
        pad[halo : halo + 128, :] = value.reshape(128, 128).T
        pad[halo + 128 : 2 * halo + 128, :] = jnp.zeros((halo, 128), F32)
        pad[0:halo, :] = jnp.zeros((halo, 128), F32)
        for d in range(ND):
            out_ref[d, off : off + rows, :] = pad[T_OWN * d : T_OWN * d + rows, :]

    put(src_ref[1], SRC1)
    put(damp_ref[...], DAMP)
    put(term_ref[...], TERM)
    put(src_ref[0], SRC0)
    yl = lax.broadcasted_iota(jnp.int32, (8, 128), 1) % 16
    row = lax.broadcasted_iota(jnp.int32, (8, 128), 0)
    react = []
    for k in range(2):
        react.append(jnp.where(yl < 8, stiff_ref[reg_ref[k, 0, 0]], stiff_ref[reg_ref[k, 0, 1]]))
    tail = jnp.where(row == 0, react[1], react[0])
    for d in range(ND):
        out_ref[d, REACT : REACT + 8, :] = tail


def spread(scr, recv_ref, off, rows):
    for s in range(ND):
        scr[pl.ds(s, rows, stride=8), :] = recv_ref[s, off : off + rows, :]
    return scr[0 : rows * 8, :].reshape(rows, 8, 128)


def first_kernel(recv_ref, out_ref, inv_ref, rhs_ref, fac_ref, scr_d, scr_t, scr1, scr0):
    d = space()
    react1 = recv_ref[:, REACT, :]
    react0 = recv_ref[:, REACT + 1, :]
    damp = spread(scr_d, recv_ref, DAMP[0], DAMP[1])
    inside = row_mask(40, 12, d)
    zero = jnp.zeros((40, 8, 128), F32)
    inv1 = jnp.where(inside[9:31], 1.0 / (CENTRE + (react1[None] + damp[9:31])), zero[9:31])
    inv0 = jnp.where(inside[5:35], 1.0 / (CENTRE + (react0[None] + damp[5:35])), zero[5:35])
    inv_ref[...] = inv1
    fac_ref[...] = 1.0 / (1.0 + 2.0 * (react0[None] + damp[12:28]))
    spread(scr1, recv_ref, SRC1[0], SRC1[1])

    @pl.when(is_last_slab())
    def _():
        wide = jnp.where(inside, 1.0 / (CENTRE + (react1[None] + damp)), zero)
        v = phi(spread(scr_t, recv_ref, TERM[0], TERM[1]), wide[1:39])
        scr1[...] = scr1[...] + v.reshape(256, 128)

    rhs = phi(scr1[...].reshape(32, 8, 128), inv0)
    rhs = rhs + spread(scr0, recv_ref, SRC0[0], SRC0[1])
    rhs_ref[...] = rhs[4:20]
    scr_t[0 : 24 * 8, :] = rhs.reshape(24 * 8, 128)
    for s in range(ND):
        out_ref[32 * s : 32 * s + 24, :] = scr_t[pl.ds(s, 24, stride=8), :]
        out_ref[32 * s + 24 : 32 * s + 32, :] = jnp.broadcast_to(recv_ref[s, REACT + 1 : REACT + 2, :], (8, 128))


def own_damp(recv1_ref):
    return recv1_ref[lax.axis_index("tl"), DAMP[0] + 8 : DAMP[0] + 32, :]


def compose_kernel(recv1_ref, recv_ref, out_ref):
    damp = own_damp(recv1_ref)
    carry = recv_ref[32 * (NL - 1) : 32 * (NL - 1) + 24, :]
    for j in range(NL - 2, -1, -1):
        react = recv_ref[32 * j + 24 : 32 * j + 25, :]
        carry = carry / (1.0 + 2.0 * (react + damp)) + recv_ref[32 * j : 32 * j + 24, :]
    group = lax.broadcasted_iota(jnp.int32, (1, 128), 1) // 16
    tail = recv_ref[24:25, :]
    for j in range(1, NL):
        tail = jnp.where(group == j, recv_ref[32 * j + 24 : 32 * j + 25, :], tail)
    for h in range(NH):
        out_ref[25 * h : 25 * h + 24, :] = carry
        out_ref[25 * h + 24 : 25 * h + 25, :] = tail


def scan_kernel(recv1_ref, recv2_ref, recv_ref, out_ref):
    me = lax.axis_index("th")
    damp = own_damp(recv1_ref)
    carry = jnp.zeros((24, 128), F32)
    own_lanes = lax.broadcasted_iota(jnp.int32, (8, 128), 1) // 16 == lax.broadcasted_iota(jnp.int32, (8, 128), 0)
    for h in range(NH - 1, 0, -1):
        react = jnp.where(own_lanes, recv_ref[25 * h + 24 : 25 * h + 25, :], jnp.zeros((8, 128), F32))
        for shift in (16, 32, 64):
            react = react + pltpu.roll(react, shift, 1)
        den = None
        for j in range(NL):
            term = 1.0 + 2.0 * (react[j : j + 1] + damp)
            den = term if den is None else den * term
        carry = jnp.where(h > me, carry / den + recv_ref[25 * h : 25 * h + 24, :], carry)
    for j in range(NL - 1, -1, -1):
        out_ref[24 * j : 24 * j + 24, :] = carry
        react = recv2_ref[32 * j + 24 : 32 * j + 25, :]
        carry = carry / (1.0 + 2.0 * (react + damp)) + recv2_ref[32 * j : 32 * j + 24, :]


def final_kernel(recv1_ref, inv_ref, rhs_ref, fac_ref, recv_ref, out_ref, scr):
    last = is_last_slab()
    for s in range(ND):
        scr[pl.ds(s, 24, stride=8), :] = recv_ref[24 * s : 24 * s + 24, :]
    incoming = scr[...].reshape(24, 8, 128)
    own = fac_ref[...] * incoming[4:20] + rhs_ref[...]
    scr[0:128, :] = own.reshape(128, 128)
    for s in range(ND):
        out_ref[s, 0:16, :] = scr[pl.ds(s, 16, stride=8), :]
    for s in range(ND):
        scr[pl.ds(s, 24, stride=8), :] = recv1_ref[s, TERM[0] + 8 : TERM[0] + 32, :]
    w = phi(jnp.where(last, scr[...].reshape(24, 8, 128), incoming), inv_ref[...])
    scr[0:128, :] = w.reshape(128, 128)
    for s in range(ND):
        out_ref[s, 16:32, :] = scr[pl.ds(s, 16, stride=8), :] + recv1_ref[s, SRC1[0] + 8 : SRC1[0] + 24, :]


def unpack_kernel(recv_ref, state_ref, adj_ref, part_ref):
    total = None
    for k in range(2):
        rows = jnp.concatenate([recv_ref[s, 16 * k : 16 * k + 16, :] for s in range(ND)], axis=0)
        value = rows.T
        adj_ref[k] = value.reshape(8, 16, 128)
        prod = value * state_ref[k].reshape(128, 128)
        total = prod if total is None else total + prod
    part_ref[...] = -total


def sum_kernel(recv_ref, out_ref):
    total = recv_ref[0:16, :]
    for i in range(1, 8):
        total = total + recv_ref[16 * i : 16 * i + 16, :]
    for i in range(8):
        out_ref[16 * i : 16 * i + 16, :] = total


VM = pl.BlockSpec(memory_space=pltpu.VMEM)
SM = pl.BlockSpec(memory_space=pltpu.SMEM)
INTERPRET = False


def near(value):
    return pltpu.with_memory_space_constraint(value, pltpu.VMEM)


def call(kernel, outs, in_specs, scratch=(), name=None):
    shapes = [jax.ShapeDtypeStruct(s[1:], F32) if s[0] is None else pltpu.VMEM(s, F32) for s in outs]
    single = len(shapes) == 1
    return pl.pallas_call(
        kernel,
        out_shape=shapes[0] if single else shapes,
        in_specs=in_specs,
        out_specs=VM if single else [VM] * len(shapes),
        scratch_shapes=list(scratch),
        name=name,
        interpret=INTERPRET,
    )


def shards(sources, forward_states, terminal, damping, contact_stiff, regions):
    def exchange(v, axes):
        rows = v.size // 1024
        slots = v.reshape(8, rows, 128) if rows % 8 == 0 else v.reshape(8, 1, rows * 128)
        return lax.all_to_all(slots, axes, 0, 0, tiled=True).reshape(v.shape)

    def scratch(rows):
        return pltpu.VMEM((rows, 128), F32)

    send1 = call(pack_kernel, [(ND, ROWS1, 128)], [SM, SM, VM, VM, VM], [scratch(152)], "pack")(
        contact_stiff, regions, sources, damping, terminal
    )
    recv1 = near(exchange(send1, ("sx", "sy")))
    send2, inv1, rhs, fac = call(
        first_kernel,
        [(256, 128), (22, 8, 128), (16, 8, 128), (16, 8, 128)],
        [VM],
        [scratch(320), scratch(320), scratch(256), scratch(192)],
        "first",
    )(recv1)
    inv1, rhs, fac = near(inv1), near(rhs), near(fac)
    recv2 = near(exchange(send2, "tl"))
    send_h = call(compose_kernel, [(200, 128)], [VM, VM], name="compose")(recv1, recv2)
    recv_h = near(exchange(send_h, "th"))
    send3 = call(scan_kernel, [(192, 128)], [VM] * 3, name="scan")(recv1, recv2, recv_h)
    recv3 = near(exchange(send3, "tl"))
    send4 = call(final_kernel, [(ND, 32, 128)], [VM] * 5, [scratch(192)], "final")(recv1, inv1, rhs, fac, recv3)
    recv4 = near(exchange(send4, ("sx", "sy")))
    adjoint, part = call(unpack_kernel, [(None, 2, 8, 16, 128), (128, 128)], [VM, VM], name="unpack")(
        recv4, near(forward_states)
    )
    for axis in ("tl", "th"):
        part = call(sum_kernel, [(128, 128)], [VM], name="sum_" + axis)(near(exchange(part, axis)))
    grad = exchange(part, "tl")
    return adjoint, grad.reshape(8, 16, 128)


def solution(mesh):
    split = Mesh(mesh.devices.reshape(NH, NL, 4, 2), ("th", "tl", "sx", "sy"))
    tm = ("th", "tl")
    in_specs = (
        P(tm, "sx", "sy", None),
        P(tm, "sx", "sy", None),
        P("sx", "sy", None),
        P("sx", "sy", None),
        P(),
        P(tm, "sx", "sy"),
    )
    out_specs = (P(tm, "sx", "sy", None), P("sx", "sy", None))
    return jax.shard_map(shards, mesh=split, in_specs=in_specs, out_specs=out_specs, check_vma=False)
```

```python
import jax
import jax.numpy as jnp
from jax import lax
from jax.experimental import pallas as pl
from jax.experimental.pallas import tpu as pltpu
from jax.sharding import Mesh
from jax.sharding import PartitionSpec as P

F32 = jnp.float32
COUPLING = 0.5
CENTRE = 1.0 + 6.0 * COUPLING

NH, NL, ND = 8, 8, 8

T_OWN = 16
SRC1 = (0, 32, 8)
DAMP = (32, 40, 12)
TERM = (72, 40, 12)
SRC0 = (112, 24, 4)
REACT = 136
ROWS1 = 144


def xy_neighbours(f):
    sub = lax.broadcasted_iota(jnp.int32, f.shape, 1)
    lane = lax.broadcasted_iota(jnp.int32, f.shape, 2)
    yl = lane % 16
    xp = pltpu.roll(f, 112, 2)
    xm = pltpu.roll(f, 16, 2)
    xpc = pltpu.roll(xp, 6, 1)
    xmc = pltpu.roll(xm, 2, 1)
    zero = jnp.zeros_like(f)
    total = jnp.where(lane < 112, xp, jnp.where(sub < 6, xpc, zero))
    total = total + jnp.where(lane >= 16, xm, jnp.where(sub >= 2, xmc, zero))
    yp = pltpu.roll(f, 127, 2)
    ym = pltpu.roll(f, 1, 2)
    even = (sub % 2) == 0
    ypc = pltpu.roll(pltpu.roll(f, 15, 2), 7, 1)
    ymc = pltpu.roll(pltpu.roll(f, 113, 2), 1, 1)
    total = total + jnp.where(yl < 15, yp, jnp.where(even, ypc, zero))
    total = total + jnp.where(yl > 0, ym, jnp.where(even, zero, ymc))
    return total


def phi(b, inv):
    n = b.shape[0]
    x = b
    for s in range(1, 5):
        nb = x[2:] + x[:-2] + xy_neighbours(x[1:-1])
        rows = slice(s, n - s)
        x = (b[rows] + COUPLING * nb) * inv[s - 1 : n - s - 1]
    return x


def row_mask(rows, halo, d):
    t = lax.broadcasted_iota(jnp.int32, (rows, 8, 128), 0) + d * T_OWN - halo
    return (t >= 0) & (t < 128)


def is_last_slab():
    return (lax.axis_index("th") == NH - 1) & (lax.axis_index("tl") == NL - 1)


def space():
    return lax.axis_index("sx") * 2 + lax.axis_index("sy")


def pack_kernel(stiff_ref, reg_ref, src_ref, damp_ref, term_ref, state_ref, out_ref, st_ref, pad, turn):
    def put(value, spec):
        off, rows, halo = spec
        pad[halo : halo + 128, :] = value.reshape(128, 128).T
        pad[halo + 128 : 2 * halo + 128, :] = jnp.zeros((halo, 128), F32)
        pad[0:halo, :] = jnp.zeros((halo, 128), F32)
        for d in range(ND):
            out_ref[d, off : off + rows, :] = pad[T_OWN * d : T_OWN * d + rows, :]

    put(src_ref[1], SRC1)
    put(damp_ref[...], DAMP)
    put(term_ref[...], TERM)
    put(src_ref[0], SRC0)
    yl = lax.broadcasted_iota(jnp.int32, (8, 128), 1) % 16
    row = lax.broadcasted_iota(jnp.int32, (8, 128), 0)
    react = []
    for k in range(2):
        react.append(jnp.where(yl < 8, stiff_ref[reg_ref[k, 0, 0]], stiff_ref[reg_ref[k, 0, 1]]))
    tail = jnp.where(row == 0, react[1], react[0])
    for d in range(ND):
        out_ref[d, REACT : REACT + 8, :] = tail
    for k in range(2):
        turn[...] = state_ref[k].reshape(128, 128).T
        for q in range(NL):
            for r in range(2):
                st_ref[pl.ds(32 * q + 2 * k + r, 8, stride=4), :] = turn[pl.ds(2 * q + r, 8, stride=16), :]


def spread(scr, recv_ref, off, rows):
    for s in range(ND):
        scr[pl.ds(s, rows, stride=8), :] = recv_ref[s, off : off + rows, :]
    return scr[0 : rows * 8, :].reshape(rows, 8, 128)


def first_kernel(recv_ref, st_ref, out_ref, inv_ref, rhs_ref, fac_ref, src_ref, scr_d, scr_t, scr1, scr0):
    d = space()
    react1 = recv_ref[:, REACT, :]
    react0 = recv_ref[:, REACT + 1, :]
    damp = spread(scr_d, recv_ref, DAMP[0], DAMP[1])
    inside = row_mask(40, 12, d)
    zero = jnp.zeros((40, 8, 128), F32)
    inv1 = jnp.where(inside[9:31], 1.0 / (CENTRE + (react1[None] + damp[9:31])), zero[9:31])
    inv0 = jnp.where(inside[5:35], 1.0 / (CENTRE + (react0[None] + damp[5:35])), zero[5:35])
    inv_ref[...] = inv1
    fac_ref[...] = 1.0 / (1.0 + 2.0 * (react0[None] + damp[12:28]))
    src_ref[...] = spread(scr1, recv_ref, SRC1[0], SRC1[1])[8:24]

    @pl.when(is_last_slab())
    def _():
        wide = jnp.where(inside, 1.0 / (CENTRE + (react1[None] + damp)), zero)
        v = phi(spread(scr_t, recv_ref, TERM[0], TERM[1]), wide[1:39])
        scr1[...] = scr1[...] + v.reshape(256, 128)

    rhs = phi(scr1[...].reshape(32, 8, 128), inv0)
    rhs = rhs + spread(scr0, recv_ref, SRC0[0], SRC0[1])
    rhs_ref[...] = rhs[4:20]
    scr_t[0 : 24 * 8, :] = rhs.reshape(24 * 8, 128)
    for s in range(ND):
        out_ref[64 * s : 64 * s + 24, :] = scr_t[pl.ds(s, 24, stride=8), :]
        out_ref[64 * s + 24 : 64 * s + 32, :] = jnp.broadcast_to(recv_ref[s, REACT + 1 : REACT + 2, :], (8, 128))
        out_ref[64 * s + 32 : 64 * s + 64, :] = st_ref[32 * s : 32 * s + 32, :]


def own_damp(recv1_ref):
    return recv1_ref[lax.axis_index("tl"), DAMP[0] + 8 : DAMP[0] + 32, :]


def compose_kernel(recv1_ref, recv_ref, out_ref):
    damp = own_damp(recv1_ref)
    carry = recv_ref[64 * (NL - 1) : 64 * (NL - 1) + 24, :]
    for j in range(NL - 2, -1, -1):
        react = recv_ref[64 * j + 24 : 64 * j + 25, :]
        carry = carry / (1.0 + 2.0 * (react + damp)) + recv_ref[64 * j : 64 * j + 24, :]
    group = lax.broadcasted_iota(jnp.int32, (1, 128), 1) // 16
    tail = recv_ref[24:25, :]
    for j in range(1, NL):
        tail = jnp.where(group == j, recv_ref[64 * j + 24 : 64 * j + 25, :], tail)
    for h in range(NH):
        out_ref[25 * h : 25 * h + 24, :] = carry
        out_ref[25 * h + 24 : 25 * h + 25, :] = tail


def scan_kernel(recv1_ref, recv2_ref, recv_ref, out_ref):
    me = lax.axis_index("th")
    damp = own_damp(recv1_ref)
    carry = jnp.zeros((24, 128), F32)
    own_lanes = lax.broadcasted_iota(jnp.int32, (8, 128), 1) // 16 == lax.broadcasted_iota(jnp.int32, (8, 128), 0)
    for h in range(NH - 1, 0, -1):
        react = jnp.where(own_lanes, recv_ref[25 * h + 24 : 25 * h + 25, :], jnp.zeros((8, 128), F32))
        for shift in (16, 32, 64):
            react = react + pltpu.roll(react, shift, 1)
        den = None
        for j in range(NL):
            term = 1.0 + 2.0 * (react[j : j + 1] + damp)
            den = term if den is None else den * term
        carry = jnp.where(h > me, carry / den + recv_ref[25 * h : 25 * h + 24, :], carry)
    for j in range(NL - 1, -1, -1):
        out_ref[24 * j : 24 * j + 24, :] = carry
        react = recv2_ref[64 * j + 24 : 64 * j + 25, :]
        carry = carry / (1.0 + 2.0 * (react + damp)) + recv2_ref[64 * j : 64 * j + 24, :]


def final_kernel(recv1_ref, inv_ref, rhs_ref, fac_ref, src_ref, recv_ref, out_ref, scr, layers):
    for s in range(ND):
        scr[pl.ds(s, 24, stride=8), :] = recv_ref[24 * s : 24 * s + 24, :]
    own = fac_ref[...] * scr[32:160, :].reshape(16, 8, 128) + rhs_ref[...]
    layers[0] = own.reshape(128, 128)

    @pl.when(is_last_slab())
    def _():
        for s in range(ND):
            scr[pl.ds(s, 24, stride=8), :] = recv1_ref[s, TERM[0] + 8 : TERM[0] + 32, :]

    w = phi(scr[...].reshape(24, 8, 128), inv_ref[...]) + src_ref[...]
    layers[1] = w.reshape(128, 128)
    for s in range(ND):
        for k in range(2):
            for r in range(2):
                out_ref[pl.ds(4 * s + 2 * k + r, 8, stride=32), :] = layers[k, pl.ds(8 * r + s, 8, stride=16), :]


def product_kernel(recv2_ref, recv_ref, out_ref, scr):
    total = recv_ref[0:32, :] * recv2_ref[32:64, :]
    for j in range(1, NL):
        total = total + recv_ref[32 * j : 32 * j + 32, :] * recv2_ref[64 * j + 32 : 64 * j + 64, :]
    scr[...] = -total
    for r in range(2):
        rows = scr[pl.ds(r, 8, stride=4), :] + scr[pl.ds(2 + r, 8, stride=4), :]
        for h in range(NH):
            out_ref[16 * h + 8 * r : 16 * h + 8 * r + 8, :] = rows


def join_kernel(layers_ref, recv_ref, out_ref):
    total = recv_ref[0:16, :]
    for h in range(1, NH):
        total = total + recv_ref[16 * h : 16 * h + 16, :]
    for j in range(NL):
        out_ref[48 * j : 48 * j + 32, :] = layers_ref[32 * j : 32 * j + 32, :]
        out_ref[48 * j + 32 : 48 * j + 48, :] = total


def unpack_kernel(recv_ref, adj_ref, grad_ref, scr):
    for q in range(NL):
        for r in range(2):
            rows = pl.ds(2 * q + r, 8, stride=16)
            for k in range(2):
                scr[k, rows, :] = recv_ref[pl.ds(48 * q + 2 * k + r, 8, stride=4), :]
            scr[2, rows, :] = recv_ref[48 * q + 32 + 8 * r : 48 * q + 40 + 8 * r, :]
    for k in range(2):
        adj_ref[k] = scr[k].T.reshape(8, 16, 128)
    grad_ref[...] = scr[2].T.reshape(8, 16, 128)


VM = pl.BlockSpec(memory_space=pltpu.VMEM)
SM = pl.BlockSpec(memory_space=pltpu.SMEM)
INTERPRET = False


def near(value):
    return pltpu.with_memory_space_constraint(value, pltpu.VMEM)


def call(kernel, outs, in_specs, scratch=(), name=None):
    shapes = [jax.ShapeDtypeStruct(s[1:], F32) if s[0] is None else pltpu.VMEM(s, F32) for s in outs]
    single = len(shapes) == 1
    return pl.pallas_call(
        kernel,
        out_shape=shapes[0] if single else shapes,
        in_specs=in_specs,
        out_specs=VM if single else [VM] * len(shapes),
        scratch_shapes=list(scratch),
        name=name,
        interpret=INTERPRET,
    )


def shards(sources, forward_states, terminal, damping, contact_stiff, regions):
    def exchange(v, axes, slots=8):
        rows = v.size // (128 * slots)
        whole = rows % 8 == 0 or rows == 4
        v3 = v.reshape(slots, rows, 128) if whole else v.reshape(slots, 1, rows * 128)
        return near(lax.all_to_all(v3, axes, 0, 0, tiled=True).reshape(v.shape))

    def scratch(rows):
        return pltpu.VMEM((rows, 128), F32)

    xy, group = ("sx", "sy"), ("tl", "sx", "sy")
    send1, pieces = call(
        pack_kernel, [(ND, ROWS1, 128), (256, 128)], [SM, SM] + [VM] * 4, [scratch(152), scratch(128)], "pack"
    )(contact_stiff, regions, sources, damping, terminal, forward_states)
    recv1 = exchange(send1, xy)
    send2, inv1, rhs, fac, src1 = call(
        first_kernel,
        [(512, 128), (22, 8, 128), (16, 8, 128), (16, 8, 128), (16, 8, 128)],
        [VM, VM],
        [scratch(320), scratch(320), scratch(256), scratch(192)],
        "first",
    )(recv1, near(pieces))
    recv2 = exchange(send2, "tl")
    send_h = call(compose_kernel, [(200, 128)], [VM, VM], name="compose")(recv1, recv2)
    recv_h = exchange(send_h, "th")
    send3 = call(scan_kernel, [(192, 128)], [VM] * 3, name="scan")(recv1, recv2, recv_h)
    recv3 = exchange(send3, "tl")
    layers = call(
        final_kernel, [(256, 128)], [VM] * 6, [scratch(192), pltpu.VMEM((2, 128, 128), F32)], "final"
    )(recv1, near(inv1), near(rhs), near(fac), near(src1), recv3)
    layers = exchange(layers, group, 64)
    part = call(product_kernel, [(128, 128)], [VM, VM], [scratch(32)], "product")(recv2, layers)
    part = exchange(part, "th")
    joined = call(join_kernel, [(384, 128)], [VM, VM], name="join")(layers, part)
    joined = exchange(joined, "tl")
    return tuple(
        call(
            unpack_kernel,
            [(None, 2, 8, 16, 128), (None, 8, 16, 128)],
            [VM],
            [pltpu.VMEM((3, 128, 128), F32)],
            "unpack",
        )(joined)
    )


def solution(mesh):
    split = Mesh(mesh.devices.reshape(NH, NL, 4, 2), ("th", "tl", "sx", "sy"))
    tm = ("th", "tl")
    in_specs = (
        P(tm, "sx", "sy", None),
        P(tm, "sx", "sy", None),
        P("sx", "sy", None),
        P("sx", "sy", None),
        P(),
        P(tm, "sx", "sy"),
    )
    out_specs = (P(tm, "sx", "sy", None), P("sx", "sy", None))
    return jax.shard_map(shards, mesh=split, in_specs=in_specs, out_specs=out_specs, check_vma=False)
```

```python
import jax
import jax.numpy as jnp
from jax import lax
from jax.experimental import pallas as pl
from jax.experimental.pallas import tpu as pltpu
from jax.sharding import Mesh
from jax.sharding import PartitionSpec as P

F32 = jnp.float32
COUPLING = 0.5
CENTRE = 1.0 + 6.0 * COUPLING

NH, NL, ND = 8, 8, 8

T_OWN = 16
SRC1 = (0, 32, 8)
TERM = (32, 40, 12)
SRC0 = (72, 24, 4)
DAMP = (96, 38, 11)
REACT = 134
ROWS1 = 136


def xy_neighbours(f):
    sub = lax.broadcasted_iota(jnp.int32, f.shape, 1)
    lane = lax.broadcasted_iota(jnp.int32, f.shape, 2)
    yl = lane % 16
    xp = pltpu.roll(f, 112, 2)
    xm = pltpu.roll(f, 16, 2)
    xpc = pltpu.roll(xp, 6, 1)
    xmc = pltpu.roll(xm, 2, 1)
    zero = jnp.zeros_like(f)
    total = jnp.where(lane < 112, xp, jnp.where(sub < 6, xpc, zero))
    total = total + jnp.where(lane >= 16, xm, jnp.where(sub >= 2, xmc, zero))
    yp = pltpu.roll(f, 127, 2)
    ym = pltpu.roll(f, 1, 2)
    even = (sub % 2) == 0
    ypc = pltpu.roll(pltpu.roll(f, 15, 2), 7, 1)
    ymc = pltpu.roll(pltpu.roll(f, 113, 2), 1, 1)
    total = total + jnp.where(yl < 15, yp, jnp.where(even, ypc, zero))
    total = total + jnp.where(yl > 0, ym, jnp.where(even, zero, ymc))
    return total


def phi(b, inv):
    n = b.shape[0]
    x = b
    for s in range(1, 5):
        nb = x[2:] + x[:-2] + xy_neighbours(x[1:-1])
        rows = slice(s, n - s)
        x = (b[rows] + COUPLING * nb) * inv[s - 1 : n - s - 1]
    return x


def row_mask(rows, halo, d):
    t = lax.broadcasted_iota(jnp.int32, (rows, 8, 128), 0) + d * T_OWN - halo
    return (t >= 0) & (t < 128)


def is_last_slab():
    return (lax.axis_index("th") == NH - 1) & (lax.axis_index("tl") == NL - 1)


def space():
    return lax.axis_index("sx") * 2 + lax.axis_index("sy")


def pack_kernel(stiff_ref, reg_ref, src_hbm, damp_hbm, term_hbm, state_hbm, out_ref, st_ref, pad, turn, arr, sem):
    parts = (src_hbm.at[1], damp_hbm, term_hbm, src_hbm.at[0], state_hbm.at[0], state_hbm.at[1])
    copies = [pltpu.make_async_copy(part, arr.at[i], sem.at[i]) for i, part in enumerate(parts)]
    for copy in copies:
        copy.start()

    yl = lax.broadcasted_iota(jnp.int32, (2, 128), 1) % 16
    row = lax.broadcasted_iota(jnp.int32, (2, 128), 0)
    react = []
    for k in range(2):
        react.append(jnp.where(yl < 8, stiff_ref[reg_ref[k, 0, 0]], stiff_ref[reg_ref[k, 0, 1]]))
    tail = jnp.where(row == 0, react[1], react[0])
    for d in range(ND):
        out_ref[d, REACT : REACT + 2, :] = tail

    for i, (off, rows, halo) in enumerate((SRC1, DAMP, TERM, SRC0)):
        pad[i, 0:halo, :] = jnp.zeros((halo, 128), F32)
        pad[i, halo + 128 : 2 * halo + 128, :] = jnp.zeros((halo, 128), F32)
        copies[i].wait()
        pad[i, halo : halo + 128, :] = arr[i].reshape(128, 128).T
        for d in range(ND):
            out_ref[d, off : off + rows, :] = pad[i, T_OWN * d : T_OWN * d + rows, :]

    for k in range(2):
        copies[4 + k].wait()
        turn[k] = arr[4 + k].reshape(128, 128).T
        for q in range(NL):
            for r in range(2):
                st_ref[pl.ds(32 * q + 2 * k + r, 8, stride=4), :] = turn[k, pl.ds(2 * q + r, 8, stride=16), :]


def spread(scr, recv_ref, off, rows):
    for s in range(ND):
        scr[pl.ds(s, rows, stride=8), :] = recv_ref[s, off : off + rows, :]
    return scr[0 : rows * 8, :].reshape(rows, 8, 128)


def first_kernel(recv_ref, st_ref, out_ref, inv_ref, rhs_ref, fac_ref, src_ref, scr_d, scr_t, scr1, scr0):
    d = space()
    react1 = recv_ref[:, REACT, :]
    react0 = recv_ref[:, REACT + 1, :]
    damp = spread(scr_d, recv_ref, DAMP[0], DAMP[1])
    inside = row_mask(38, 11, d)
    zero = jnp.zeros((38, 8, 128), F32)
    inv1 = jnp.where(inside[8:30], 1.0 / (CENTRE + (react1[None] + damp[8:30])), zero[8:30])
    inv0 = jnp.where(inside[4:34], 1.0 / (CENTRE + (react0[None] + damp[4:34])), zero[4:34])
    inv_ref[...] = inv1
    fac_ref[...] = 1.0 / (1.0 + 2.0 * (react0[None] + damp[11:27]))
    src_ref[...] = spread(scr1, recv_ref, SRC1[0], SRC1[1])[8:24]

    @pl.when(is_last_slab())
    def _():
        wide = jnp.where(inside, 1.0 / (CENTRE + (react1[None] + damp)), zero)
        v = phi(spread(scr_t, recv_ref, TERM[0], TERM[1]), wide)
        scr1[...] = scr1[...] + v.reshape(256, 128)

    rhs = phi(scr1[...].reshape(32, 8, 128), inv0)
    rhs = rhs + spread(scr0, recv_ref, SRC0[0], SRC0[1])
    rhs_ref[...] = rhs[4:20]
    scr_t[0 : 24 * 8, :] = rhs.reshape(24 * 8, 128)
    for s in range(ND):
        out_ref[64 * s : 64 * s + 24, :] = scr_t[pl.ds(s, 24, stride=8), :]
        out_ref[64 * s + 24 : 64 * s + 32, :] = jnp.broadcast_to(recv_ref[s, REACT + 1 : REACT + 2, :], (8, 128))
        out_ref[64 * s + 32 : 64 * s + 64, :] = st_ref[32 * s : 32 * s + 32, :]


def own_damp(recv1_ref):
    return recv1_ref[lax.axis_index("tl"), DAMP[0] + 7 : DAMP[0] + 31, :]


def compose_kernel(recv1_ref, recv_ref, out_ref):
    damp = own_damp(recv1_ref)
    carry = recv_ref[64 * (NL - 1) : 64 * (NL - 1) + 24, :]
    for j in range(NL - 2, -1, -1):
        react = recv_ref[64 * j + 24 : 64 * j + 25, :]
        carry = carry / (1.0 + 2.0 * (react + damp)) + recv_ref[64 * j : 64 * j + 24, :]
    group = lax.broadcasted_iota(jnp.int32, (1, 128), 1) // 16
    tail = recv_ref[24:25, :]
    for j in range(1, NL):
        tail = jnp.where(group == j, recv_ref[64 * j + 24 : 64 * j + 25, :], tail)
    for h in range(NH):
        out_ref[25 * h : 25 * h + 24, :] = carry
        out_ref[25 * h + 24 : 25 * h + 25, :] = tail


def scan_kernel(recv1_ref, recv2_ref, recv_ref, out_ref):
    me = lax.axis_index("th")
    damp = own_damp(recv1_ref)
    carry = jnp.zeros((24, 128), F32)
    own_lanes = lax.broadcasted_iota(jnp.int32, (8, 128), 1) // 16 == lax.broadcasted_iota(jnp.int32, (8, 128), 0)
    for h in range(NH - 1, 0, -1):
        react = jnp.where(own_lanes, recv_ref[25 * h + 24 : 25 * h + 25, :], jnp.zeros((8, 128), F32))
        for shift in (16, 32, 64):
            react = react + pltpu.roll(react, shift, 1)
        den = None
        for j in range(NL):
            term = 1.0 + 2.0 * (react[j : j + 1] + damp)
            den = term if den is None else den * term
        carry = jnp.where(h > me, carry / den + recv_ref[25 * h : 25 * h + 24, :], carry)
    for j in range(NL - 1, -1, -1):
        out_ref[24 * j : 24 * j + 24, :] = carry
        react = recv2_ref[64 * j + 24 : 64 * j + 25, :]
        carry = carry / (1.0 + 2.0 * (react + damp)) + recv2_ref[64 * j : 64 * j + 24, :]


def final_kernel(recv1_ref, inv_ref, rhs_ref, fac_ref, src_ref, recv_ref, out_ref, scr, layers):
    for s in range(ND):
        scr[pl.ds(s, 24, stride=8), :] = recv_ref[24 * s : 24 * s + 24, :]
    own = fac_ref[...] * scr[32:160, :].reshape(16, 8, 128) + rhs_ref[...]
    layers[0] = own.reshape(128, 128)

    @pl.when(is_last_slab())
    def _():
        for s in range(ND):
            scr[pl.ds(s, 24, stride=8), :] = recv1_ref[s, TERM[0] + 8 : TERM[0] + 32, :]

    w = phi(scr[...].reshape(24, 8, 128), inv_ref[...]) + src_ref[...]
    layers[1] = w.reshape(128, 128)
    for s in range(ND):
        for k in range(2):
            for r in range(2):
                out_ref[pl.ds(4 * s + 2 * k + r, 8, stride=32), :] = layers[k, pl.ds(8 * r + s, 8, stride=16), :]


def product_kernel(recv2_ref, recv_ref, out_ref, scr):
    total = recv_ref[0:32, :] * recv2_ref[32:64, :]
    for j in range(1, NL):
        total = total + recv_ref[32 * j : 32 * j + 32, :] * recv2_ref[64 * j + 32 : 64 * j + 64, :]
    scr[...] = -total
    for r in range(2):
        rows = scr[pl.ds(r, 8, stride=4), :] + scr[pl.ds(2 + r, 8, stride=4), :]
        for h in range(NH):
            out_ref[16 * h + 8 * r : 16 * h + 8 * r + 8, :] = rows


def join_kernel(layers_ref, recv_ref, out_ref):
    total = recv_ref[0:16, :]
    for h in range(1, NH):
        total = total + recv_ref[16 * h : 16 * h + 16, :]
    for j in range(NL):
        out_ref[48 * j : 48 * j + 32, :] = layers_ref[32 * j : 32 * j + 32, :]
        out_ref[48 * j + 32 : 48 * j + 48, :] = total


def unpack_kernel(recv_ref, adj_hbm, grad_hbm, scr, out, sem):
    dests = (adj_hbm.at[0], adj_hbm.at[1], grad_hbm)
    copies = []
    for k, dest in enumerate(dests):
        for q in range(NL):
            for r in range(2):
                rows = pl.ds(2 * q + r, 8, stride=16)
                if k < 2:
                    scr[k, rows, :] = recv_ref[pl.ds(48 * q + 2 * k + r, 8, stride=4), :]
                else:
                    scr[k, rows, :] = recv_ref[48 * q + 32 + 8 * r : 48 * q + 40 + 8 * r, :]
        out[k] = scr[k].T.reshape(8, 16, 128)
        copies.append(pltpu.make_async_copy(out.at[k], dest, sem.at[k]))
        copies[k].start()
    for copy in copies:
        copy.wait()


VM = pl.BlockSpec(memory_space=pltpu.VMEM)
SM = pl.BlockSpec(memory_space=pltpu.SMEM)
HB = pl.BlockSpec(memory_space=pl.ANY)
INTERPRET = False


def near(value):
    return pltpu.with_memory_space_constraint(value, pltpu.VMEM)


def call(kernel, outs, in_specs, scratch=(), name=None):
    shapes = [jax.ShapeDtypeStruct(s[1:], F32) if s[0] is None else pltpu.VMEM(s, F32) for s in outs]
    single = len(shapes) == 1
    specs = [HB if s[0] is None else VM for s in outs]
    return pl.pallas_call(
        kernel,
        out_shape=shapes[0] if single else shapes,
        in_specs=in_specs,
        out_specs=specs[0] if single else specs,
        scratch_shapes=list(scratch),
        name=name,
        interpret=INTERPRET,
    )


def shards(sources, forward_states, terminal, damping, contact_stiff, regions):
    def exchange(v, axes, slots=8):
        rows = v.size // (128 * slots)
        whole = rows % 8 == 0 or rows == 4
        v3 = v.reshape(slots, rows, 128) if whole else v.reshape(slots, 1, rows * 128)
        return near(lax.all_to_all(v3, axes, 0, 0, tiled=True).reshape(v.shape))

    def scratch(rows):
        return pltpu.VMEM((rows, 128), F32)

    xy, group = ("sx", "sy"), ("tl", "sx", "sy")
    send1, pieces = call(
        pack_kernel,
        [(ND, ROWS1, 128), (256, 128)],
        [SM, SM] + [HB] * 4,
        [
            pltpu.VMEM((4, 152, 128), F32),
            pltpu.VMEM((2, 128, 128), F32),
            pltpu.VMEM((6, 8, 16, 128), F32),
            pltpu.SemaphoreType.DMA((6,)),
        ],
        "pack",
    )(contact_stiff, regions, sources, damping, terminal, forward_states)
    recv1 = exchange(send1, xy)
    send2, inv1, rhs, fac, src1 = call(
        first_kernel,
        [(512, 128), (22, 8, 128), (16, 8, 128), (16, 8, 128), (16, 8, 128)],
        [VM, VM],
        [scratch(320), scratch(320), scratch(256), scratch(192)],
        "first",
    )(recv1, near(pieces))
    recv2 = exchange(send2, "tl")
    send_h = call(compose_kernel, [(200, 128)], [VM, VM], name="compose")(recv1, recv2)
    recv_h = exchange(send_h, "th")
    send3 = call(scan_kernel, [(192, 128)], [VM] * 3, name="scan")(recv1, recv2, recv_h)
    recv3 = exchange(send3, "tl")
    layers = call(
        final_kernel, [(256, 128)], [VM] * 6, [scratch(192), pltpu.VMEM((2, 128, 128), F32)], "final"
    )(recv1, near(inv1), near(rhs), near(fac), near(src1), recv3)
    layers = exchange(layers, group, 64)
    part = call(product_kernel, [(128, 128)], [VM, VM], [scratch(32)], "product")(recv2, layers)
    part = exchange(part, "th")
    joined = call(join_kernel, [(384, 128)], [VM, VM], name="join")(layers, part)
    joined = exchange(joined, "tl")
    return tuple(
        call(
            unpack_kernel,
            [(None, 2, 8, 16, 128), (None, 8, 16, 128)],
            [VM],
            [pltpu.VMEM((3, 128, 128), F32), pltpu.VMEM((3, 8, 16, 128), F32), pltpu.SemaphoreType.DMA((3,))],
            "unpack",
        )(joined)
    )


def solution(mesh):
    split = Mesh(mesh.devices.reshape(NH, NL, 4, 2), ("th", "tl", "sx", "sy"))
    tm = ("th", "tl")
    in_specs = (
        P(tm, "sx", "sy", None),
        P(tm, "sx", "sy", None),
        P("sx", "sy", None),
        P("sx", "sy", None),
        P(),
        P(tm, "sx", "sy"),
    )
    out_specs = (P(tm, "sx", "sy", None), P("sx", "sy", None))
    return jax.shard_map(shards, mesh=split, in_specs=in_specs, out_specs=out_specs, check_vma=False)
```

```python
import jax
import jax.numpy as jnp
from jax import lax
from jax.experimental import pallas as pl
from jax.experimental.pallas import tpu as pltpu
from jax.sharding import Mesh
from jax.sharding import PartitionSpec as P

F32 = jnp.float32
COUPLING = 0.5
CENTRE = 1.0 + 6.0 * COUPLING

NH, NL, ND = 8, 8, 8

T_OWN = 16
SRC1 = (0, 32, 8)
TERM = (32, 40, 12)
SRC0 = (72, 24, 4)
DAMP = (96, 38, 11)
REACT = 134
ROWS1 = 136


def xy_neighbours(f):
    sub = lax.broadcasted_iota(jnp.int32, f.shape, 1)
    lane = lax.broadcasted_iota(jnp.int32, f.shape, 2)
    yl = lane % 16
    xp = pltpu.roll(f, 112, 2)
    xm = pltpu.roll(f, 16, 2)
    xpc = pltpu.roll(xp, 6, 1)
    xmc = pltpu.roll(xm, 2, 1)
    zero = jnp.zeros_like(f)
    total = jnp.where(lane < 112, xp, jnp.where(sub < 6, xpc, zero))
    total = total + jnp.where(lane >= 16, xm, jnp.where(sub >= 2, xmc, zero))
    yp = pltpu.roll(f, 127, 2)
    ym = pltpu.roll(f, 1, 2)
    even = (sub % 2) == 0
    ypc = pltpu.roll(pltpu.roll(f, 15, 2), 7, 1)
    ymc = pltpu.roll(pltpu.roll(f, 113, 2), 1, 1)
    total = total + jnp.where(yl < 15, yp, jnp.where(even, ypc, zero))
    total = total + jnp.where(yl > 0, ym, jnp.where(even, zero, ymc))
    return total


def phi(b, inv):
    n = b.shape[0]
    x = b
    for s in range(1, 5):
        nb = x[2:] + x[:-2] + xy_neighbours(x[1:-1])
        rows = slice(s, n - s)
        x = (b[rows] + COUPLING * nb) * inv[s - 1 : n - s - 1]
    return x


def row_mask(rows, halo, d):
    t = lax.broadcasted_iota(jnp.int32, (rows, 8, 128), 0) + d * T_OWN - halo
    return (t >= 0) & (t < 128)


def is_last_slab():
    return (lax.axis_index("th") == NH - 1) & (lax.axis_index("tl") == NL - 1)


def space():
    return lax.axis_index("sx") * 2 + lax.axis_index("sy")


def pack_kernel(stiff_ref, reg_ref, src_ref, damp_ref, term_ref, state_ref, out_ref, st_ref, pad, turn):
    def put(value, spec):
        off, rows, halo = spec
        pad[halo : halo + 128, :] = value.reshape(128, 128).T
        pad[halo + 128 : 2 * halo + 128, :] = jnp.zeros((halo, 128), F32)
        pad[0:halo, :] = jnp.zeros((halo, 128), F32)
        for d in range(ND):
            out_ref[d, off : off + rows, :] = pad[T_OWN * d : T_OWN * d + rows, :]

    put(src_ref[1], SRC1)
    put(damp_ref[...], DAMP)
    put(term_ref[...], TERM)
    put(src_ref[0], SRC0)
    yl = lax.broadcasted_iota(jnp.int32, (2, 128), 1) % 16
    row = lax.broadcasted_iota(jnp.int32, (2, 128), 0)
    react = []
    for k in range(2):
        react.append(jnp.where(yl < 8, stiff_ref[reg_ref[k, 0, 0]], stiff_ref[reg_ref[k, 0, 1]]))
    tail = jnp.where(row == 0, react[1], react[0])
    for d in range(ND):
        out_ref[d, REACT : REACT + 2, :] = tail
    for k in range(2):
        turn[...] = state_ref[k].reshape(128, 128).T
        for q in range(NL):
            for r in range(2):
                st_ref[pl.ds(32 * q + 2 * k + r, 8, stride=4), :] = turn[pl.ds(2 * q + r, 8, stride=16), :]


def spread(scr, recv_ref, off, rows):
    for s in range(ND):
        scr[pl.ds(s, rows, stride=8), :] = recv_ref[s, off : off + rows, :]
    return scr[0 : rows * 8, :].reshape(rows, 8, 128)


def first_kernel(recv_ref, st_ref, out_ref, inv_ref, rhs_ref, fac_ref, src_ref, scr_d, scr_t, scr1, scr0):
    d = space()
    react1 = recv_ref[:, REACT, :]
    react0 = recv_ref[:, REACT + 1, :]
    damp = spread(scr_d, recv_ref, DAMP[0], DAMP[1])
    inside = row_mask(38, 11, d)
    zero = jnp.zeros((38, 8, 128), F32)
    inv1 = jnp.where(inside[8:30], 1.0 / (CENTRE + (react1[None] + damp[8:30])), zero[8:30])
    inv0 = jnp.where(inside[4:34], 1.0 / (CENTRE + (react0[None] + damp[4:34])), zero[4:34])
    inv_ref[...] = inv1
    fac_ref[...] = 1.0 / (1.0 + 2.0 * (react0[None] + damp[11:27]))
    src_ref[...] = spread(scr1, recv_ref, SRC1[0], SRC1[1])[8:24]

    @pl.when(is_last_slab())
    def _():
        wide = jnp.where(inside, 1.0 / (CENTRE + (react1[None] + damp)), zero)
        v = phi(spread(scr_t, recv_ref, TERM[0], TERM[1]), wide)
        scr1[...] = scr1[...] + v.reshape(256, 128)

    rhs = phi(scr1[...].reshape(32, 8, 128), inv0)
    rhs = rhs + spread(scr0, recv_ref, SRC0[0], SRC0[1])
    rhs_ref[...] = rhs[4:20]
    scr_t[0 : 24 * 8, :] = rhs.reshape(24 * 8, 128)
    for s in range(ND):
        out_ref[64 * s : 64 * s + 24, :] = scr_t[pl.ds(s, 24, stride=8), :]
        out_ref[64 * s + 24 : 64 * s + 32, :] = jnp.broadcast_to(recv_ref[s, REACT + 1 : REACT + 2, :], (8, 128))
        out_ref[64 * s + 32 : 64 * s + 64, :] = st_ref[32 * s : 32 * s + 32, :]


def own_damp(recv1_ref):
    return recv1_ref[lax.axis_index("tl"), DAMP[0] + 7 : DAMP[0] + 31, :]


def compose_kernel(recv1_ref, recv_ref, out_ref):
    damp = own_damp(recv1_ref)
    carry = recv_ref[64 * (NL - 1) : 64 * (NL - 1) + 24, :]
    for j in range(NL - 2, -1, -1):
        react = recv_ref[64 * j + 24 : 64 * j + 25, :]
        carry = carry / (1.0 + 2.0 * (react + damp)) + recv_ref[64 * j : 64 * j + 24, :]
    group = lax.broadcasted_iota(jnp.int32, (1, 128), 1) // 16
    tail = recv_ref[24:25, :]
    for j in range(1, NL):
        tail = jnp.where(group == j, recv_ref[64 * j + 24 : 64 * j + 25, :], tail)
    for h in range(NH):
        out_ref[25 * h : 25 * h + 24, :] = carry
        out_ref[25 * h + 24 : 25 * h + 25, :] = tail


def scan_kernel(recv1_ref, recv2_ref, recv_ref, out_ref):
    me = lax.axis_index("th")
    damp = own_damp(recv1_ref)
    carry = jnp.zeros((24, 128), F32)
    own_lanes = lax.broadcasted_iota(jnp.int32, (8, 128), 1) // 16 == lax.broadcasted_iota(jnp.int32, (8, 128), 0)
    for h in range(NH - 1, 0, -1):
        react = jnp.where(own_lanes, recv_ref[25 * h + 24 : 25 * h + 25, :], jnp.zeros((8, 128), F32))
        for shift in (16, 32, 64):
            react = react + pltpu.roll(react, shift, 1)
        den = None
        for j in range(NL):
            term = 1.0 + 2.0 * (react[j : j + 1] + damp)
            den = term if den is None else den * term
        carry = jnp.where(h > me, carry / den + recv_ref[25 * h : 25 * h + 24, :], carry)
    for j in range(NL - 1, -1, -1):
        out_ref[24 * j : 24 * j + 24, :] = carry
        react = recv2_ref[64 * j + 24 : 64 * j + 25, :]
        carry = carry / (1.0 + 2.0 * (react + damp)) + recv2_ref[64 * j : 64 * j + 24, :]


def final_kernel(recv1_ref, inv_ref, rhs_ref, fac_ref, src_ref, recv_ref, out_ref, scr, layers):
    for s in range(ND):
        scr[pl.ds(s, 24, stride=8), :] = recv_ref[24 * s : 24 * s + 24, :]
    own = fac_ref[...] * scr[32:160, :].reshape(16, 8, 128) + rhs_ref[...]
    layers[0] = own.reshape(128, 128)

    @pl.when(is_last_slab())
    def _():
        for s in range(ND):
            scr[pl.ds(s, 24, stride=8), :] = recv1_ref[s, TERM[0] + 8 : TERM[0] + 32, :]

    w = phi(scr[...].reshape(24, 8, 128), inv_ref[...]) + src_ref[...]
    layers[1] = w.reshape(128, 128)
    for s in range(ND):
        for k in range(2):
            for r in range(2):
                out_ref[pl.ds(4 * s + 2 * k + r, 8, stride=32), :] = layers[k, pl.ds(8 * r + s, 8, stride=16), :]


def product_kernel(recv2_ref, recv_ref, out_ref, scr):
    total = recv_ref[0:32, :] * recv2_ref[32:64, :]
    for j in range(1, NL):
        total = total + recv_ref[32 * j : 32 * j + 32, :] * recv2_ref[64 * j + 32 : 64 * j + 64, :]
    scr[...] = -total
    for r in range(2):
        rows = scr[pl.ds(r, 8, stride=4), :] + scr[pl.ds(2 + r, 8, stride=4), :]
        for h in range(NH):
            out_ref[16 * h + 8 * r : 16 * h + 8 * r + 8, :] = rows


def join_kernel(layers_ref, recv_ref, out_ref):
    total = recv_ref[0:16, :]
    for h in range(1, NH):
        total = total + recv_ref[16 * h : 16 * h + 16, :]
    for j in range(NL):
        out_ref[48 * j : 48 * j + 32, :] = layers_ref[32 * j : 32 * j + 32, :]
        out_ref[48 * j + 32 : 48 * j + 48, :] = total


def unpack_kernel(recv_ref, adj_ref, grad_ref, scr):
    for q in range(NL):
        for r in range(2):
            rows = pl.ds(2 * q + r, 8, stride=16)
            for k in range(2):
                scr[k, rows, :] = recv_ref[pl.ds(48 * q + 2 * k + r, 8, stride=4), :]
            scr[2, rows, :] = recv_ref[48 * q + 32 + 8 * r : 48 * q + 40 + 8 * r, :]
    for k in range(2):
        adj_ref[k] = scr[k].T.reshape(8, 16, 128)
    grad_ref[...] = scr[2].T.reshape(8, 16, 128)


VM = pl.BlockSpec(memory_space=pltpu.VMEM)
SM = pl.BlockSpec(memory_space=pltpu.SMEM)
INTERPRET = False


def near(value):
    return pltpu.with_memory_space_constraint(value, pltpu.VMEM)


def call(kernel, outs, in_specs, scratch=(), name=None):
    shapes = [jax.ShapeDtypeStruct(s[1:], F32) if s[0] is None else pltpu.VMEM(s, F32) for s in outs]
    single = len(shapes) == 1
    return pl.pallas_call(
        kernel,
        out_shape=shapes[0] if single else shapes,
        in_specs=in_specs,
        out_specs=VM if single else [VM] * len(shapes),
        scratch_shapes=list(scratch),
        name=name,
        interpret=INTERPRET,
    )


def shards(sources, forward_states, terminal, damping, contact_stiff, regions):
    def exchange(v, axes, slots=8):
        rows = v.size // (128 * slots)
        whole = rows % 8 == 0 or rows == 4
        v3 = v.reshape(slots, rows, 128) if whole else v.reshape(slots, 1, rows * 128)
        return near(lax.all_to_all(v3, axes, 0, 0, tiled=True).reshape(v.shape))

    def scratch(rows):
        return pltpu.VMEM((rows, 128), F32)

    xy, group = ("sx", "sy"), ("tl", "sx", "sy")
    send1, pieces = call(
        pack_kernel, [(ND, ROWS1, 128), (256, 128)], [SM, SM] + [VM] * 4, [scratch(152), scratch(128)], "pack"
    )(contact_stiff, regions, sources, damping, terminal, forward_states)
    recv1 = exchange(send1, xy)
    send2, inv1, rhs, fac, src1 = call(
        first_kernel,
        [(512, 128), (22, 8, 128), (16, 8, 128), (16, 8, 128), (16, 8, 128)],
        [VM, VM],
        [scratch(320), scratch(320), scratch(256), scratch(192)],
        "first",
    )(recv1, near(pieces))
    recv2 = exchange(send2, "tl")
    send_h = call(compose_kernel, [(200, 128)], [VM, VM], name="compose")(recv1, recv2)
    recv_h = exchange(send_h, "th")
    send3 = call(scan_kernel, [(192, 128)], [VM] * 3, name="scan")(recv1, recv2, recv_h)
    recv3 = exchange(send3, "tl")
    layers = call(
        final_kernel, [(256, 128)], [VM] * 6, [scratch(192), pltpu.VMEM((2, 128, 128), F32)], "final"
    )(recv1, near(inv1), near(rhs), near(fac), near(src1), recv3)
    layers = exchange(layers, group, 64)
    part = call(product_kernel, [(128, 128)], [VM, VM], [scratch(32)], "product")(recv2, layers)
    part = exchange(part, "th")
    joined = call(join_kernel, [(384, 128)], [VM, VM], name="join")(layers, part)
    joined = exchange(joined, "tl")
    return tuple(
        call(
            unpack_kernel,
            [(None, 2, 8, 16, 128), (None, 8, 16, 128)],
            [VM],
            [pltpu.VMEM((3, 128, 128), F32)],
            "unpack",
        )(joined)
    )


def solution(mesh):
    split = Mesh(mesh.devices.reshape(NH, NL, 4, 2), ("th", "tl", "sx", "sy"))
    tm = ("th", "tl")
    in_specs = (
        P(tm, "sx", "sy", None),
        P(tm, "sx", "sy", None),
        P("sx", "sy", None),
        P("sx", "sy", None),
        P(),
        P(tm, "sx", "sy"),
    )
    out_specs = (P(tm, "sx", "sy", None), P("sx", "sy", None))
    return jax.shard_map(shards, mesh=split, in_specs=in_specs, out_specs=out_specs, check_vma=False)
```

```python
import jax
import jax.numpy as jnp
from jax import lax
from jax.experimental import pallas as pl
from jax.experimental.pallas import tpu as pltpu
from jax.sharding import Mesh
from jax.sharding import PartitionSpec as P

F32 = jnp.float32
COUPLING = 0.5
CENTRE = 1.0 + 6.0 * COUPLING

NH, NL, ND = 8, 8, 8

T_OWN = 16
SRC1 = (0, 32, 8)
TERM = (32, 40, 12)
SRC0 = (72, 24, 4)
DAMP = (96, 38, 11)
REACT = 134
ROWS1 = 136


def neighbours(field):
    rows = field[0].shape[0]
    zero = jnp.zeros_like(field[0])
    lane = lax.broadcasted_iota(jnp.int32, field[0].shape, 1)
    yl = lane % 16
    after = [pltpu.roll(f, 112, 1) for f in field] + [zero, zero]
    before = [zero, zero] + [pltpu.roll(f, 16, 1) for f in field]
    out = []
    for s, f in enumerate(field):
        total = pltpu.roll(f, 1, 0) + pltpu.roll(f, rows - 1, 0)
        total = total + jnp.where(lane < 112, after[s], after[s + 2])
        total = total + jnp.where(lane >= 16, before[s + 2], before[s])
        other = pltpu.roll(field[s ^ 1], 15 if s % 2 == 0 else 113, 1)
        total = total + jnp.where(yl < 15, pltpu.roll(f, 127, 1), other if s % 2 == 0 else zero)
        total = total + jnp.where(yl > 0, pltpu.roll(f, 1, 1), zero if s % 2 == 0 else other)
        out.append(total)
    return out


def phi(b, inv):
    x = b
    for _ in range(4):
        x = [(b[s] + COUPLING * n) * inv[s] for s, n in enumerate(neighbours(x))]
    return x


def row_mask(rows, halo, d):
    t = lax.broadcasted_iota(jnp.int32, (rows, 128), 0) + d * T_OWN - halo
    return (t >= 0) & (t < 128)


def inverse(recv_ref, step, halo, d):
    rows = T_OWN + 2 * halo
    first = DAMP[0] + DAMP[2] - halo
    inside = row_mask(rows, halo, d)
    out = []
    for s in range(ND):
        react = recv_ref[s, REACT + 1 - step : REACT + 2 - step, :]
        diag = CENTRE + (react + recv_ref[s, first : first + rows, :])
        out.append(jnp.where(inside, 1.0 / diag, jnp.zeros_like(diag)))
    return out


def is_last_slab():
    return (lax.axis_index("th") == NH - 1) & (lax.axis_index("tl") == NL - 1)


def space():
    return lax.axis_index("sx") * 2 + lax.axis_index("sy")


def pack_kernel(stiff_ref, reg_ref, src_ref, damp_ref, term_ref, state_ref, out_ref, st_ref, pad, turn):
    def put(value, spec):
        off, rows, halo = spec
        pad[halo : halo + 128, :] = value.reshape(128, 128).T
        pad[halo + 128 : 2 * halo + 128, :] = jnp.zeros((halo, 128), F32)
        pad[0:halo, :] = jnp.zeros((halo, 128), F32)
        for d in range(ND):
            out_ref[d, off : off + rows, :] = pad[T_OWN * d : T_OWN * d + rows, :]

    put(src_ref[1], SRC1)
    put(damp_ref[...], DAMP)
    put(term_ref[...], TERM)
    put(src_ref[0], SRC0)
    yl = lax.broadcasted_iota(jnp.int32, (2, 128), 1) % 16
    row = lax.broadcasted_iota(jnp.int32, (2, 128), 0)
    react = []
    for k in range(2):
        react.append(jnp.where(yl < 8, stiff_ref[reg_ref[k, 0, 0]], stiff_ref[reg_ref[k, 0, 1]]))
    tail = jnp.where(row == 0, react[1], react[0])
    for d in range(ND):
        out_ref[d, REACT : REACT + 2, :] = tail
    for k in range(2):
        turn[...] = state_ref[k].reshape(128, 128).T
        for q in range(NL):
            for r in range(2):
                st_ref[pl.ds(32 * q + 2 * k + r, 8, stride=4), :] = turn[pl.ds(2 * q + r, 8, stride=16), :]


def first_kernel(recv_ref, st_ref, out_ref, inv_ref, rhs_ref, fac_ref, scr):
    d = space()
    for s in range(ND):
        scr[s] = recv_ref[s, SRC1[0] : SRC1[0] + 32, :]

    @pl.when(is_last_slab())
    def _():
        edge = jnp.zeros((1, 128), F32)
        inv = [jnp.concatenate([edge, v, edge], axis=0) for v in inverse(recv_ref, 1, 11, d)]
        v = phi([recv_ref[s, TERM[0] : TERM[0] + 40, :] for s in range(ND)], inv)
        for s in range(ND):
            scr[s] = scr[s] + v[s][4:36]

    inv1 = inverse(recv_ref, 1, 4, d)
    rhs = phi([scr[s] for s in range(ND)], inverse(recv_ref, 0, 8, d))
    for s in range(ND):
        react0 = recv_ref[s, REACT + 1 : REACT + 2, :]
        inv_ref[s] = inv1[s]
        fac_ref[s] = 1.0 / (1.0 + 2.0 * (react0 + recv_ref[s, DAMP[0] + 11 : DAMP[0] + 27, :]))
        part = rhs[s][4:28] + recv_ref[s, SRC0[0] : SRC0[0] + 24, :]
        rhs_ref[s] = part[4:20]
        out_ref[64 * s : 64 * s + 24, :] = part
        out_ref[64 * s + 24 : 64 * s + 32, :] = jnp.broadcast_to(react0, (8, 128))
        out_ref[64 * s + 32 : 64 * s + 64, :] = st_ref[32 * s : 32 * s + 32, :]


def own_damp(recv1_ref):
    return recv1_ref[lax.axis_index("tl"), DAMP[0] + 7 : DAMP[0] + 31, :]


def compose_kernel(recv1_ref, recv_ref, out_ref):
    damp = own_damp(recv1_ref)
    carry = recv_ref[64 * (NL - 1) : 64 * (NL - 1) + 24, :]
    for j in range(NL - 2, -1, -1):
        react = recv_ref[64 * j + 24 : 64 * j + 25, :]
        carry = carry / (1.0 + 2.0 * (react + damp)) + recv_ref[64 * j : 64 * j + 24, :]
    group = lax.broadcasted_iota(jnp.int32, (1, 128), 1) // 16
    tail = recv_ref[24:25, :]
    for j in range(1, NL):
        tail = jnp.where(group == j, recv_ref[64 * j + 24 : 64 * j + 25, :], tail)
    for h in range(NH):
        out_ref[25 * h : 25 * h + 24, :] = carry
        out_ref[25 * h + 24 : 25 * h + 25, :] = tail


def scan_kernel(recv1_ref, recv2_ref, recv_ref, out_ref):
    me = lax.axis_index("th")
    damp = own_damp(recv1_ref)
    carry = jnp.zeros((24, 128), F32)
    own_lanes = lax.broadcasted_iota(jnp.int32, (8, 128), 1) // 16 == lax.broadcasted_iota(jnp.int32, (8, 128), 0)
    for h in range(NH - 1, 0, -1):
        react = jnp.where(own_lanes, recv_ref[25 * h + 24 : 25 * h + 25, :], jnp.zeros((8, 128), F32))
        for shift in (16, 32, 64):
            react = react + pltpu.roll(react, shift, 1)
        den = None
        for j in range(NL):
            term = 1.0 + 2.0 * (react[j : j + 1] + damp)
            den = term if den is None else den * term
        carry = jnp.where(h > me, carry / den + recv_ref[25 * h : 25 * h + 24, :], carry)
    for j in range(NL - 1, -1, -1):
        out_ref[24 * j : 24 * j + 24, :] = carry
        react = recv2_ref[64 * j + 24 : 64 * j + 25, :]
        carry = carry / (1.0 + 2.0 * (react + damp)) + recv2_ref[64 * j : 64 * j + 24, :]


def final_kernel(recv1_ref, inv_ref, rhs_ref, fac_ref, recv_ref, out_ref, layers):
    last = is_last_slab()
    field = []
    for s in range(ND):
        incoming = recv_ref[24 * s : 24 * s + 24, :]
        layers[0, 16 * s : 16 * s + 16, :] = fac_ref[s] * incoming[4:20] + rhs_ref[s]
        field.append(jnp.where(last, recv1_ref[s, TERM[0] + 8 : TERM[0] + 32, :], incoming))
    w = phi(field, [inv_ref[s] for s in range(ND)])
    for s in range(ND):
        layers[1, 16 * s : 16 * s + 16, :] = w[s][4:20] + recv1_ref[s, SRC1[0] + 8 : SRC1[0] + 24, :]
    for s in range(ND):
        for k in range(2):
            for r in range(2):
                out_ref[pl.ds(4 * s + 2 * k + r, 8, stride=32), :] = layers[k, pl.ds(16 * s + r, 8, stride=2), :]


def product_kernel(recv2_ref, recv_ref, out_ref, scr):
    total = recv_ref[0:32, :] * recv2_ref[32:64, :]
    for j in range(1, NL):
        total = total + recv_ref[32 * j : 32 * j + 32, :] * recv2_ref[64 * j + 32 : 64 * j + 64, :]
    scr[...] = -total
    for r in range(2):
        rows = scr[pl.ds(r, 8, stride=4), :] + scr[pl.ds(2 + r, 8, stride=4), :]
        for h in range(NH):
            out_ref[16 * h + 8 * r : 16 * h + 8 * r + 8, :] = rows


def join_kernel(layers_ref, recv_ref, out_ref):
    total = recv_ref[0:16, :]
    for h in range(1, NH):
        total = total + recv_ref[16 * h : 16 * h + 16, :]
    for j in range(NL):
        out_ref[48 * j : 48 * j + 32, :] = layers_ref[32 * j : 32 * j + 32, :]
        out_ref[48 * j + 32 : 48 * j + 48, :] = total


def unpack_kernel(recv_ref, adj_ref, grad_ref, scr):
    for q in range(NL):
        for r in range(2):
            rows = pl.ds(2 * q + r, 8, stride=16)
            for k in range(2):
                scr[k, rows, :] = recv_ref[pl.ds(48 * q + 2 * k + r, 8, stride=4), :]
            scr[2, rows, :] = recv_ref[48 * q + 32 + 8 * r : 48 * q + 40 + 8 * r, :]
    for k in range(2):
        adj_ref[k] = scr[k].T.reshape(8, 16, 128)
    grad_ref[...] = scr[2].T.reshape(8, 16, 128)


VM = pl.BlockSpec(memory_space=pltpu.VMEM)
SM = pl.BlockSpec(memory_space=pltpu.SMEM)
INTERPRET = False


def near(value):
    return pltpu.with_memory_space_constraint(value, pltpu.VMEM)


def call(kernel, outs, in_specs, scratch=(), name=None):
    shapes = [jax.ShapeDtypeStruct(s[1:], F32) if s[0] is None else pltpu.VMEM(s, F32) for s in outs]
    single = len(shapes) == 1
    return pl.pallas_call(
        kernel,
        out_shape=shapes[0] if single else shapes,
        in_specs=in_specs,
        out_specs=VM if single else [VM] * len(shapes),
        scratch_shapes=list(scratch),
        name=name,
        interpret=INTERPRET,
    )


def shards(sources, forward_states, terminal, damping, contact_stiff, regions):
    def exchange(v, axes, slots=8):
        rows = v.size // (128 * slots)
        whole = rows % 8 == 0 or rows == 4
        v3 = v.reshape(slots, rows, 128) if whole else v.reshape(slots, 1, rows * 128)
        return near(lax.all_to_all(v3, axes, 0, 0, tiled=True).reshape(v.shape))

    def scratch(rows):
        return pltpu.VMEM((rows, 128), F32)

    xy, group = ("sx", "sy"), ("tl", "sx", "sy")
    send1, pieces = call(
        pack_kernel, [(ND, ROWS1, 128), (256, 128)], [SM, SM] + [VM] * 4, [scratch(152), scratch(128)], "pack"
    )(contact_stiff, regions, sources, damping, terminal, forward_states)
    recv1 = exchange(send1, xy)
    send2, inv1, rhs, fac = call(
        first_kernel,
        [(512, 128), (8, 24, 128), (8, 16, 128), (8, 16, 128)],
        [VM, VM],
        [pltpu.VMEM((8, 32, 128), F32)],
        "first",
    )(recv1, near(pieces))
    recv2 = exchange(send2, "tl")
    send_h = call(compose_kernel, [(200, 128)], [VM, VM], name="compose")(recv1, recv2)
    recv_h = exchange(send_h, "th")
    send3 = call(scan_kernel, [(192, 128)], [VM] * 3, name="scan")(recv1, recv2, recv_h)
    recv3 = exchange(send3, "tl")
    layers = call(final_kernel, [(256, 128)], [VM] * 5, [pltpu.VMEM((2, 128, 128), F32)], "final")(
        recv1, near(inv1), near(rhs), near(fac), recv3
    )
    layers = exchange(layers, group, 64)
    part = call(product_kernel, [(128, 128)], [VM, VM], [scratch(32)], "product")(recv2, layers)
    part = exchange(part, "th")
    joined = call(join_kernel, [(384, 128)], [VM, VM], name="join")(layers, part)
    joined = exchange(joined, "tl")
    return tuple(
        call(
            unpack_kernel,
            [(None, 2, 8, 16, 128), (None, 8, 16, 128)],
            [VM],
            [pltpu.VMEM((3, 128, 128), F32)],
            "unpack",
        )(joined)
    )


def solution(mesh):
    split = Mesh(mesh.devices.reshape(NH, NL, 4, 2), ("th", "tl", "sx", "sy"))
    tm = ("th", "tl")
    in_specs = (
        P(tm, "sx", "sy", None),
        P(tm, "sx", "sy", None),
        P("sx", "sy", None),
        P("sx", "sy", None),
        P(),
        P(tm, "sx", "sy"),
    )
    out_specs = (P(tm, "sx", "sy", None), P("sx", "sy", None))
    return jax.shard_map(shards, mesh=split, in_specs=in_specs, out_specs=out_specs, check_vma=False)
```

```python
import jax
import jax.numpy as jnp
from jax import lax
from jax.experimental import pallas as pl
from jax.experimental.pallas import tpu as pltpu
from jax.sharding import Mesh
from jax.sharding import PartitionSpec as P

F32 = jnp.float32
COUPLING = 0.5
CENTRE = 1.0 + 6.0 * COUPLING

NH, NL, ND = 8, 8, 8

T_OWN = 16
SRC1 = (0, 32, 8)
TERM = (32, 40, 12)
SRC0 = (72, 24, 4)
DAMP = (96, 38, 11)
REACT = 134
ROWS1 = 136


def neighbours(field):
    rows = field[0].shape[0]
    zero = jnp.zeros_like(field[0])
    lane = lax.broadcasted_iota(jnp.int32, field[0].shape, 1)
    yl = lane % 16
    after = [pltpu.roll(f, 112, 1) for f in field] + [zero, zero]
    before = [zero, zero] + [pltpu.roll(f, 16, 1) for f in field]
    out = []
    for s, f in enumerate(field):
        total = pltpu.roll(f, 1, 0) + pltpu.roll(f, rows - 1, 0)
        total = total + jnp.where(lane < 112, after[s], after[s + 2])
        total = total + jnp.where(lane >= 16, before[s + 2], before[s])
        other = pltpu.roll(field[s ^ 1], 15 if s % 2 == 0 else 113, 1)
        total = total + jnp.where(yl < 15, pltpu.roll(f, 127, 1), other if s % 2 == 0 else zero)
        total = total + jnp.where(yl > 0, pltpu.roll(f, 1, 1), zero if s % 2 == 0 else other)
        out.append(total)
    return out


def phi(b, inv):
    x = b
    for _ in range(4):
        x = [(b[s] + COUPLING * n) * inv[s] for s, n in enumerate(neighbours(x))]
    return x


def row_mask(rows, halo, d):
    t = lax.broadcasted_iota(jnp.int32, (rows, 128), 0) + d * T_OWN - halo
    return (t >= 0) & (t < 128)


def inverse(recv_ref, step, halo, d):
    rows = T_OWN + 2 * halo
    first = DAMP[0] + DAMP[2] - halo
    inside = row_mask(rows, halo, d)
    out = []
    for s in range(ND):
        react = recv_ref[s, REACT + 1 - step : REACT + 2 - step, :]
        diag = CENTRE + (react + recv_ref[s, first : first + rows, :])
        out.append(jnp.where(inside, 1.0 / diag, jnp.zeros_like(diag)))
    return out


def is_last_slab():
    return (lax.axis_index("th") == NH - 1) & (lax.axis_index("tl") == NL - 1)


def space():
    return lax.axis_index("sx") * 2 + lax.axis_index("sy")


def pack_kernel(stiff_ref, reg_ref, src_ref, damp_ref, term_ref, state_ref, out_ref, st_ref, pad, turn):
    def put(value, spec):
        off, rows, halo = spec
        pad[halo : halo + 128, :] = value.reshape(128, 128).T
        pad[halo + 128 : 2 * halo + 128, :] = jnp.zeros((halo, 128), F32)
        pad[0:halo, :] = jnp.zeros((halo, 128), F32)
        for d in range(ND):
            out_ref[d, off : off + rows, :] = pad[T_OWN * d : T_OWN * d + rows, :]

    put(src_ref[1], SRC1)
    put(damp_ref[...], DAMP)
    put(term_ref[...], TERM)
    put(src_ref[0], SRC0)
    yl = lax.broadcasted_iota(jnp.int32, (2, 128), 1) % 16
    row = lax.broadcasted_iota(jnp.int32, (2, 128), 0)
    react = []
    for k in range(2):
        react.append(jnp.where(yl < 8, stiff_ref[reg_ref[k, 0, 0]], stiff_ref[reg_ref[k, 0, 1]]))
    tail = jnp.where(row == 0, react[1], react[0])
    for d in range(ND):
        out_ref[d, REACT : REACT + 2, :] = tail
    for k in range(2):
        turn[...] = state_ref[k].reshape(128, 128).T
        for q in range(NL):
            for r in range(2):
                st_ref[pl.ds(32 * q + 2 * k + r, 8, stride=4), :] = turn[pl.ds(2 * q + r, 8, stride=16), :]


def first_kernel(recv_ref, st_ref, out_ref, inv_ref, rhs_ref, fac_ref, scr):
    d = space()
    for s in range(ND):
        scr[s] = recv_ref[s, SRC1[0] : SRC1[0] + 32, :]

    @pl.when(is_last_slab())
    def _():
        edge = jnp.zeros((1, 128), F32)
        inv = [jnp.concatenate([edge, v, edge], axis=0) for v in inverse(recv_ref, 1, 11, d)]
        v = phi([recv_ref[s, TERM[0] : TERM[0] + 40, :] for s in range(ND)], inv)
        for s in range(ND):
            scr[s] = scr[s] + v[s][4:36]

    inv1 = inverse(recv_ref, 1, 4, d)
    rhs = phi([scr[s] for s in range(ND)], inverse(recv_ref, 0, 8, d))
    for s in range(ND):
        react0 = recv_ref[s, REACT + 1 : REACT + 2, :]
        inv_ref[s] = inv1[s]
        fac_ref[s] = 1.0 / (1.0 + 2.0 * (react0 + recv_ref[s, DAMP[0] + 11 : DAMP[0] + 27, :]))
        part = rhs[s][4:28] + recv_ref[s, SRC0[0] : SRC0[0] + 24, :]
        rhs_ref[s] = part[4:20]
        out_ref[57 * s : 57 * s + 24, :] = part
        out_ref[57 * s + 24 : 57 * s + 25, :] = react0
        out_ref[57 * s + 25 : 57 * s + 57, :] = st_ref[32 * s : 32 * s + 32, :]


def own_damp(recv1_ref):
    return recv1_ref[lax.axis_index("tl"), DAMP[0] + 7 : DAMP[0] + 31, :]


def compose_kernel(recv1_ref, recv_ref, out_ref):
    damp = own_damp(recv1_ref)
    carry = recv_ref[57 * (NL - 1) : 57 * (NL - 1) + 24, :]
    for j in range(NL - 2, -1, -1):
        react = recv_ref[57 * j + 24 : 57 * j + 25, :]
        carry = carry * (1.0 / (1.0 + 2.0 * (react + damp))) + recv_ref[57 * j : 57 * j + 24, :]
    group = lax.broadcasted_iota(jnp.int32, (1, 128), 1) // 16
    tail = recv_ref[24:25, :]
    for j in range(1, NL):
        tail = jnp.where(group == j, recv_ref[57 * j + 24 : 57 * j + 25, :], tail)
    for h in range(NH):
        out_ref[25 * h : 25 * h + 24, :] = carry
        out_ref[25 * h + 24 : 25 * h + 25, :] = tail


def scan_kernel(recv1_ref, recv2_ref, recv_ref, out_ref):
    me = lax.axis_index("th")
    damp = own_damp(recv1_ref)
    carry = jnp.zeros((24, 128), F32)
    own_lanes = lax.broadcasted_iota(jnp.int32, (8, 128), 1) // 16 == lax.broadcasted_iota(jnp.int32, (8, 128), 0)
    for h in range(NH - 1, 0, -1):
        react = jnp.where(own_lanes, recv_ref[25 * h + 24 : 25 * h + 25, :], jnp.zeros((8, 128), F32))
        for shift in (16, 32, 64):
            react = react + pltpu.roll(react, shift, 1)
        den = None
        for j in range(NL):
            term = 1.0 + 2.0 * (react[j : j + 1] + damp)
            den = term if den is None else den * term
        carry = jnp.where(h > me, carry * (1.0 / den) + recv_ref[25 * h : 25 * h + 24, :], carry)
    for j in range(NL - 1, -1, -1):
        out_ref[24 * j : 24 * j + 24, :] = carry
        react = recv2_ref[57 * j + 24 : 57 * j + 25, :]
        carry = carry * (1.0 / (1.0 + 2.0 * (react + damp))) + recv2_ref[57 * j : 57 * j + 24, :]


def final_kernel(recv1_ref, inv_ref, rhs_ref, fac_ref, recv_ref, out_ref, layers):
    last = is_last_slab()
    field = []
    for s in range(ND):
        incoming = recv_ref[24 * s : 24 * s + 24, :]
        layers[0, 16 * s : 16 * s + 16, :] = fac_ref[s] * incoming[4:20] + rhs_ref[s]
        field.append(jnp.where(last, recv1_ref[s, TERM[0] + 8 : TERM[0] + 32, :], incoming))
    w = phi(field, [inv_ref[s] for s in range(ND)])
    for s in range(ND):
        layers[1, 16 * s : 16 * s + 16, :] = w[s][4:20] + recv1_ref[s, SRC1[0] + 8 : SRC1[0] + 24, :]
    for s in range(ND):
        for k in range(2):
            for r in range(2):
                out_ref[pl.ds(4 * s + 2 * k + r, 8, stride=32), :] = layers[k, pl.ds(16 * s + r, 8, stride=2), :]


def product_kernel(recv2_ref, recv_ref, out_ref, scr):
    total = recv_ref[0:32, :] * recv2_ref[25:57, :]
    for j in range(1, NL):
        total = total + recv_ref[32 * j : 32 * j + 32, :] * recv2_ref[57 * j + 25 : 57 * j + 57, :]
    scr[...] = -total
    for r in range(2):
        rows = scr[pl.ds(r, 8, stride=4), :] + scr[pl.ds(2 + r, 8, stride=4), :]
        for h in range(NH):
            out_ref[16 * h + 8 * r : 16 * h + 8 * r + 8, :] = rows


def join_kernel(layers_ref, recv_ref, out_ref):
    total = recv_ref[0:16, :]
    for h in range(1, NH):
        total = total + recv_ref[16 * h : 16 * h + 16, :]
    for j in range(NL):
        out_ref[48 * j : 48 * j + 32, :] = layers_ref[32 * j : 32 * j + 32, :]
        out_ref[48 * j + 32 : 48 * j + 48, :] = total


def unpack_kernel(recv_ref, adj_ref, grad_ref, scr):
    for q in range(NL):
        for r in range(2):
            rows = pl.ds(2 * q + r, 8, stride=16)
            for k in range(2):
                scr[k, rows, :] = recv_ref[pl.ds(48 * q + 2 * k + r, 8, stride=4), :]
            scr[2, rows, :] = recv_ref[48 * q + 32 + 8 * r : 48 * q + 40 + 8 * r, :]
    for k in range(2):
        adj_ref[k] = scr[k].T.reshape(8, 16, 128)
    grad_ref[...] = scr[2].T.reshape(8, 16, 128)


VM = pl.BlockSpec(memory_space=pltpu.VMEM)
SM = pl.BlockSpec(memory_space=pltpu.SMEM)
INTERPRET = False


def near(value):
    return pltpu.with_memory_space_constraint(value, pltpu.VMEM)


def call(kernel, outs, in_specs, scratch=(), name=None):
    shapes = [jax.ShapeDtypeStruct(s[1:], F32) if s[0] is None else pltpu.VMEM(s, F32) for s in outs]
    single = len(shapes) == 1
    return pl.pallas_call(
        kernel,
        out_shape=shapes[0] if single else shapes,
        in_specs=in_specs,
        out_specs=VM if single else [VM] * len(shapes),
        scratch_shapes=list(scratch),
        name=name,
        interpret=INTERPRET,
    )


def shards(sources, forward_states, terminal, damping, contact_stiff, regions):
    def exchange(v, axes, slots=8):
        rows = v.size // (128 * slots)
        whole = rows % 8 == 0 or rows == 4
        v3 = v.reshape(slots, rows, 128) if whole else v.reshape(slots, 1, rows * 128)
        return near(lax.all_to_all(v3, axes, 0, 0, tiled=True).reshape(v.shape))

    def scratch(rows):
        return pltpu.VMEM((rows, 128), F32)

    xy, group = ("sx", "sy"), ("tl", "sx", "sy")
    send1, pieces = call(
        pack_kernel, [(ND, ROWS1, 128), (256, 128)], [SM, SM] + [VM] * 4, [scratch(152), scratch(128)], "pack"
    )(contact_stiff, regions, sources, damping, terminal, forward_states)
    recv1 = exchange(send1, xy)
    send2, inv1, rhs, fac = call(
        first_kernel,
        [(456, 128), (8, 24, 128), (8, 16, 128), (8, 16, 128)],
        [VM, VM],
        [pltpu.VMEM((8, 32, 128), F32)],
        "first",
    )(recv1, near(pieces))
    recv2 = exchange(send2, "tl")
    send_h = call(compose_kernel, [(200, 128)], [VM, VM], name="compose")(recv1, recv2)
    recv_h = exchange(send_h, "th")
    send3 = call(scan_kernel, [(192, 128)], [VM] * 3, name="scan")(recv1, recv2, recv_h)
    recv3 = exchange(send3, "tl")
    layers = call(final_kernel, [(256, 128)], [VM] * 5, [pltpu.VMEM((2, 128, 128), F32)], "final")(
        recv1, near(inv1), near(rhs), near(fac), recv3
    )
    layers = exchange(layers, group, 64)
    part = call(product_kernel, [(128, 128)], [VM, VM], [scratch(32)], "product")(recv2, layers)
    part = exchange(part, "th")
    joined = call(join_kernel, [(384, 128)], [VM, VM], name="join")(layers, part)
    joined = exchange(joined, "tl")
    return tuple(
        call(
            unpack_kernel,
            [(None, 2, 8, 16, 128), (None, 8, 16, 128)],
            [VM],
            [pltpu.VMEM((3, 128, 128), F32)],
            "unpack",
        )(joined)
    )


def solution(mesh):
    split = Mesh(mesh.devices.reshape(NH, NL, 4, 2), ("th", "tl", "sx", "sy"))
    tm = ("th", "tl")
    in_specs = (
        P(tm, "sx", "sy", None),
        P(tm, "sx", "sy", None),
        P("sx", "sy", None),
        P("sx", "sy", None),
        P(),
        P(tm, "sx", "sy"),
    )
    out_specs = (P(tm, "sx", "sy", None), P("sx", "sy", None))
    return jax.shard_map(shards, mesh=split, in_specs=in_specs, out_specs=out_specs, check_vma=False)
```

```python
import jax
import jax.numpy as jnp
from jax import lax
from jax.experimental import pallas as pl
from jax.experimental.pallas import tpu as pltpu
from jax.sharding import Mesh
from jax.sharding import PartitionSpec as P

F32 = jnp.float32
COUPLING = 0.5
CENTRE = 1.0 + 6.0 * COUPLING

NH, NL, ND = 8, 8, 8

T_OWN = 16
SRC1 = (0, 32, 8)
TERM = (32, 40, 12)
SRC0 = (72, 24, 4)
DAMP = (96, 38, 11)
REACT = 134
ROWS1 = 136


def neighbours(field):
    rows = field[0].shape[0]
    zero = jnp.zeros_like(field[0])
    lane = lax.broadcasted_iota(jnp.int32, field[0].shape, 1)
    yl = lane % 16
    after = [pltpu.roll(f, 112, 1) for f in field] + [zero, zero]
    before = [zero, zero] + [pltpu.roll(f, 16, 1) for f in field]
    out = []
    for s, f in enumerate(field):
        total = pltpu.roll(f, 1, 0) + pltpu.roll(f, rows - 1, 0)
        total = total + jnp.where(lane < 112, after[s], after[s + 2])
        total = total + jnp.where(lane >= 16, before[s + 2], before[s])
        other = pltpu.roll(field[s ^ 1], 15 if s % 2 == 0 else 113, 1)
        total = total + jnp.where(yl < 15, pltpu.roll(f, 127, 1), other if s % 2 == 0 else zero)
        total = total + jnp.where(yl > 0, pltpu.roll(f, 1, 1), zero if s % 2 == 0 else other)
        out.append(total)
    return out


def phi(b, inv):
    fixed = [b[s] * inv[s] for s in range(ND)]
    scale = [COUPLING * inv[s] for s in range(ND)]
    x = b
    for _ in range(4):
        x = [fixed[s] + scale[s] * n for s, n in enumerate(neighbours(x))]
    return x


def row_mask(rows, halo, d):
    t = lax.broadcasted_iota(jnp.int32, (rows, 128), 0) + d * T_OWN - halo
    return (t >= 0) & (t < 128)


def inverse(recv_ref, step, halo, d):
    rows = T_OWN + 2 * halo
    first = DAMP[0] + DAMP[2] - halo
    inside = row_mask(rows, halo, d)
    out = []
    for s in range(ND):
        react = recv_ref[s, REACT + 1 - step : REACT + 2 - step, :]
        diag = CENTRE + (react + recv_ref[s, first : first + rows, :])
        out.append(jnp.where(inside, 1.0 / diag, jnp.zeros_like(diag)))
    return out


def is_last_slab():
    return (lax.axis_index("th") == NH - 1) & (lax.axis_index("tl") == NL - 1)


def space():
    return lax.axis_index("sx") * 2 + lax.axis_index("sy")


def pack_kernel(stiff_ref, reg_ref, src_ref, damp_ref, term_ref, state_ref, out_ref, st_ref, pad, turn):
    def put(value, spec):
        off, rows, halo = spec
        pad[halo : halo + 128, :] = value.reshape(128, 128).T
        pad[halo + 128 : 2 * halo + 128, :] = jnp.zeros((halo, 128), F32)
        pad[0:halo, :] = jnp.zeros((halo, 128), F32)
        for d in range(ND):
            out_ref[d, off : off + rows, :] = pad[T_OWN * d : T_OWN * d + rows, :]

    put(src_ref[1], SRC1)
    put(damp_ref[...], DAMP)
    put(term_ref[...], TERM)
    put(src_ref[0], SRC0)
    yl = lax.broadcasted_iota(jnp.int32, (2, 128), 1) % 16
    row = lax.broadcasted_iota(jnp.int32, (2, 128), 0)
    react = []
    for k in range(2):
        react.append(jnp.where(yl < 8, stiff_ref[reg_ref[k, 0, 0]], stiff_ref[reg_ref[k, 0, 1]]))
    tail = jnp.where(row == 0, react[1], react[0])
    for d in range(ND):
        out_ref[d, REACT : REACT + 2, :] = tail
    for k in range(2):
        turn[...] = state_ref[k].reshape(128, 128).T
        for q in range(NL):
            for r in range(2):
                st_ref[pl.ds(32 * q + 2 * k + r, 8, stride=4), :] = turn[pl.ds(2 * q + r, 8, stride=16), :]


def first_kernel(recv_ref, st_ref, out_ref, inv_ref, rhs_ref, fac_ref, scr):
    d = space()
    for s in range(ND):
        scr[s] = recv_ref[s, SRC1[0] : SRC1[0] + 32, :]

    @pl.when(is_last_slab())
    def _():
        edge = jnp.zeros((1, 128), F32)
        inv = [jnp.concatenate([edge, v, edge], axis=0) for v in inverse(recv_ref, 1, 11, d)]
        v = phi([recv_ref[s, TERM[0] : TERM[0] + 40, :] for s in range(ND)], inv)
        for s in range(ND):
            scr[s] = scr[s] + v[s][4:36]

    inv1 = inverse(recv_ref, 1, 4, d)
    rhs = phi([scr[s] for s in range(ND)], inverse(recv_ref, 0, 8, d))
    for s in range(ND):
        react0 = recv_ref[s, REACT + 1 : REACT + 2, :]
        inv_ref[s] = inv1[s]
        fac_ref[s] = 1.0 / (1.0 + 2.0 * (react0 + recv_ref[s, DAMP[0] + 11 : DAMP[0] + 27, :]))
        part = rhs[s][4:28] + recv_ref[s, SRC0[0] : SRC0[0] + 24, :]
        rhs_ref[s] = part[4:20]
        out_ref[64 * s : 64 * s + 24, :] = part
        out_ref[64 * s + 24 : 64 * s + 32, :] = jnp.broadcast_to(react0, (8, 128))
        out_ref[64 * s + 32 : 64 * s + 64, :] = st_ref[32 * s : 32 * s + 32, :]


def own_damp(recv1_ref):
    return recv1_ref[lax.axis_index("tl"), DAMP[0] + 7 : DAMP[0] + 31, :]


def compose_kernel(recv1_ref, recv_ref, out_ref):
    damp = own_damp(recv1_ref)
    carry = recv_ref[64 * (NL - 1) : 64 * (NL - 1) + 24, :]
    for j in range(NL - 2, -1, -1):
        react = recv_ref[64 * j + 24 : 64 * j + 25, :]
        carry = carry / (1.0 + 2.0 * (react + damp)) + recv_ref[64 * j : 64 * j + 24, :]
    group = lax.broadcasted_iota(jnp.int32, (1, 128), 1) // 16
    tail = recv_ref[24:25, :]
    for j in range(1, NL):
        tail = jnp.where(group == j, recv_ref[64 * j + 24 : 64 * j + 25, :], tail)
    for h in range(NH):
        out_ref[25 * h : 25 * h + 24, :] = carry
        out_ref[25 * h + 24 : 25 * h + 25, :] = tail


def scan_kernel(recv1_ref, recv2_ref, recv_ref, out_ref):
    me = lax.axis_index("th")
    damp = own_damp(recv1_ref)
    carry = jnp.zeros((24, 128), F32)
    own_lanes = lax.broadcasted_iota(jnp.int32, (8, 128), 1) // 16 == lax.broadcasted_iota(jnp.int32, (8, 128), 0)
    for h in range(NH - 1, 0, -1):
        react = jnp.where(own_lanes, recv_ref[25 * h + 24 : 25 * h + 25, :], jnp.zeros((8, 128), F32))
        for shift in (16, 32, 64):
            react = react + pltpu.roll(react, shift, 1)
        den = None
        for j in range(NL):
            term = 1.0 + 2.0 * (react[j : j + 1] + damp)
            den = term if den is None else den * term
        carry = jnp.where(h > me, carry / den + recv_ref[25 * h : 25 * h + 24, :], carry)
    for j in range(NL - 1, -1, -1):
        out_ref[24 * j : 24 * j + 24, :] = carry
        react = recv2_ref[64 * j + 24 : 64 * j + 25, :]
        carry = carry / (1.0 + 2.0 * (react + damp)) + recv2_ref[64 * j : 64 * j + 24, :]


def final_kernel(recv1_ref, inv_ref, rhs_ref, fac_ref, recv_ref, out_ref, layers):
    last = is_last_slab()
    field = []
    for s in range(ND):
        incoming = recv_ref[24 * s : 24 * s + 24, :]
        layers[0, 16 * s : 16 * s + 16, :] = fac_ref[s] * incoming[4:20] + rhs_ref[s]
        field.append(jnp.where(last, recv1_ref[s, TERM[0] + 8 : TERM[0] + 32, :], incoming))
    w = phi(field, [inv_ref[s] for s in range(ND)])
    for s in range(ND):
        layers[1, 16 * s : 16 * s + 16, :] = w[s][4:20] + recv1_ref[s, SRC1[0] + 8 : SRC1[0] + 24, :]
    for s in range(ND):
        for k in range(2):
            for r in range(2):
                out_ref[pl.ds(4 * s + 2 * k + r, 8, stride=32), :] = layers[k, pl.ds(16 * s + r, 8, stride=2), :]


def product_kernel(recv2_ref, recv_ref, out_ref, scr):
    total = recv_ref[0:32, :] * recv2_ref[32:64, :]
    for j in range(1, NL):
        total = total + recv_ref[32 * j : 32 * j + 32, :] * recv2_ref[64 * j + 32 : 64 * j + 64, :]
    scr[...] = -total
    for r in range(2):
        rows = scr[pl.ds(r, 8, stride=4), :] + scr[pl.ds(2 + r, 8, stride=4), :]
        for h in range(NH):
            out_ref[16 * h + 8 * r : 16 * h + 8 * r + 8, :] = rows


def join_kernel(layers_ref, recv_ref, out_ref):
    total = recv_ref[0:16, :]
    for h in range(1, NH):
        total = total + recv_ref[16 * h : 16 * h + 16, :]
    for j in range(NL):
        out_ref[48 * j : 48 * j + 32, :] = layers_ref[32 * j : 32 * j + 32, :]
        out_ref[48 * j + 32 : 48 * j + 48, :] = total


def unpack_kernel(recv_ref, adj_ref, grad_ref, scr):
    for q in range(NL):
        for r in range(2):
            rows = pl.ds(2 * q + r, 8, stride=16)
            for k in range(2):
                scr[k, rows, :] = recv_ref[pl.ds(48 * q + 2 * k + r, 8, stride=4), :]
            scr[2, rows, :] = recv_ref[48 * q + 32 + 8 * r : 48 * q + 40 + 8 * r, :]
    for k in range(2):
        adj_ref[k] = scr[k].T.reshape(8, 16, 128)
    grad_ref[...] = scr[2].T.reshape(8, 16, 128)


VM = pl.BlockSpec(memory_space=pltpu.VMEM)
SM = pl.BlockSpec(memory_space=pltpu.SMEM)
INTERPRET = False


def near(value):
    return pltpu.with_memory_space_constraint(value, pltpu.VMEM)


def call(kernel, outs, in_specs, scratch=(), name=None):
    shapes = [jax.ShapeDtypeStruct(s[1:], F32) if s[0] is None else pltpu.VMEM(s, F32) for s in outs]
    single = len(shapes) == 1
    return pl.pallas_call(
        kernel,
        out_shape=shapes[0] if single else shapes,
        in_specs=in_specs,
        out_specs=VM if single else [VM] * len(shapes),
        scratch_shapes=list(scratch),
        name=name,
        interpret=INTERPRET,
    )


def shards(sources, forward_states, terminal, damping, contact_stiff, regions):
    def exchange(v, axes, slots=8):
        rows = v.size // (128 * slots)
        whole = rows % 8 == 0 or rows == 4
        v3 = v.reshape(slots, rows, 128) if whole else v.reshape(slots, 1, rows * 128)
        return near(lax.all_to_all(v3, axes, 0, 0, tiled=True).reshape(v.shape))

    def scratch(rows):
        return pltpu.VMEM((rows, 128), F32)

    xy, group = ("sx", "sy"), ("tl", "sx", "sy")
    send1, pieces = call(
        pack_kernel, [(ND, ROWS1, 128), (256, 128)], [SM, SM] + [VM] * 4, [scratch(152), scratch(128)], "pack"
    )(contact_stiff, regions, sources, damping, terminal, forward_states)
    recv1 = exchange(send1, xy)
    send2, inv1, rhs, fac = call(
        first_kernel,
        [(512, 128), (8, 24, 128), (8, 16, 128), (8, 16, 128)],
        [VM, VM],
        [pltpu.VMEM((8, 32, 128), F32)],
        "first",
    )(recv1, near(pieces))
    recv2 = exchange(send2, "tl")
    send_h = call(compose_kernel, [(200, 128)], [VM, VM], name="compose")(recv1, recv2)
    recv_h = exchange(send_h, "th")
    send3 = call(scan_kernel, [(192, 128)], [VM] * 3, name="scan")(recv1, recv2, recv_h)
    recv3 = exchange(send3, "tl")
    layers = call(final_kernel, [(256, 128)], [VM] * 5, [pltpu.VMEM((2, 128, 128), F32)], "final")(
        recv1, near(inv1), near(rhs), near(fac), recv3
    )
    layers = exchange(layers, group, 64)
    part = call(product_kernel, [(128, 128)], [VM, VM], [scratch(32)], "product")(recv2, layers)
    part = exchange(part, "th")
    joined = call(join_kernel, [(384, 128)], [VM, VM], name="join")(layers, part)
    joined = exchange(joined, "tl")
    return tuple(
        call(
            unpack_kernel,
            [(None, 2, 8, 16, 128), (None, 8, 16, 128)],
            [VM],
            [pltpu.VMEM((3, 128, 128), F32)],
            "unpack",
        )(joined)
    )


def solution(mesh):
    split = Mesh(mesh.devices.reshape(NH, NL, 4, 2), ("th", "tl", "sx", "sy"))
    tm = ("th", "tl")
    in_specs = (
        P(tm, "sx", "sy", None),
        P(tm, "sx", "sy", None),
        P("sx", "sy", None),
        P("sx", "sy", None),
        P(),
        P(tm, "sx", "sy"),
    )
    out_specs = (P(tm, "sx", "sy", None), P("sx", "sy", None))
    return jax.shard_map(shards, mesh=split, in_specs=in_specs, out_specs=out_specs, check_vma=False)
```

```python
import jax
import jax.numpy as jnp
from jax import lax
from jax.experimental import pallas as pl
from jax.experimental.pallas import tpu as pltpu
from jax.sharding import Mesh
from jax.sharding import PartitionSpec as P

F32 = jnp.float32
COUPLING = 0.5
CENTRE = 1.0 + 6.0 * COUPLING

NH, NL, ND = 8, 8, 8

T_OWN = 16
SRC1 = (0, 32, 8)
TERM = (32, 40, 12)
SRC0 = (72, 24, 4)
DAMP = (96, 38, 11)
REACT = 134
ROWS1 = 136


def neighbours(field):
    rows = field[0].shape[0]
    zero = jnp.zeros_like(field[0])
    lane = lax.broadcasted_iota(jnp.int32, field[0].shape, 1)
    yl = lane % 16
    after = [pltpu.roll(f, 112, 1) for f in field] + [zero, zero]
    before = [zero, zero] + [pltpu.roll(f, 16, 1) for f in field]
    out = []
    for s, f in enumerate(field):
        total = pltpu.roll(f, 1, 0) + pltpu.roll(f, rows - 1, 0)
        total = total + jnp.where(lane < 112, after[s], after[s + 2])
        total = total + jnp.where(lane >= 16, before[s + 2], before[s])
        other = pltpu.roll(field[s ^ 1], 15 if s % 2 == 0 else 113, 1)
        total = total + jnp.where(yl < 15, pltpu.roll(f, 127, 1), other if s % 2 == 0 else zero)
        total = total + jnp.where(yl > 0, pltpu.roll(f, 1, 1), zero if s % 2 == 0 else other)
        out.append(total)
    return out


def phi(b, inv):
    x = b
    for _ in range(4):
        x = [(b[s] + COUPLING * n) * inv[s] for s, n in enumerate(neighbours(x))]
    return x


def row_mask(rows, halo, d):
    t = lax.broadcasted_iota(jnp.int32, (rows, 128), 0) + d * T_OWN - halo
    return (t >= 0) & (t < 128)


def inverse(recv_ref, step, halo, d):
    rows = T_OWN + 2 * halo
    first = DAMP[0] + DAMP[2] - halo
    inside = row_mask(rows, halo, d)
    out = []
    for s in range(ND):
        react = recv_ref[s, REACT + 1 - step : REACT + 2 - step, :]
        diag = CENTRE + (react + recv_ref[s, first : first + rows, :])
        out.append(jnp.where(inside, 1.0 / diag, jnp.zeros_like(diag)))
    return out


def is_last_slab():
    return (lax.axis_index("th") == NH - 1) & (lax.axis_index("tl") == NL - 1)


def space():
    return lax.axis_index("sx") * 2 + lax.axis_index("sy")


def pack_kernel(stiff_ref, reg_ref, src_ref, damp_ref, term_ref, state_ref, out_ref, st_ref, pad, turn):
    def put(value, spec):
        off, rows, halo = spec
        pad[halo : halo + 128, :] = value.reshape(128, 128).T
        pad[halo + 128 : 2 * halo + 128, :] = jnp.zeros((halo, 128), F32)
        pad[0:halo, :] = jnp.zeros((halo, 128), F32)
        for d in range(ND):
            out_ref[d, off : off + rows, :] = pad[T_OWN * d : T_OWN * d + rows, :]

    put(src_ref[1], SRC1)
    put(damp_ref[...], DAMP)
    put(term_ref[...], TERM)
    put(src_ref[0], SRC0)
    yl = lax.broadcasted_iota(jnp.int32, (2, 128), 1) % 16
    row = lax.broadcasted_iota(jnp.int32, (2, 128), 0)
    react = []
    for k in range(2):
        react.append(jnp.where(yl < 8, stiff_ref[reg_ref[k, 0, 0]], stiff_ref[reg_ref[k, 0, 1]]))
    tail = jnp.where(row == 0, react[1], react[0])
    for d in range(ND):
        out_ref[d, REACT : REACT + 2, :] = tail
    for k in range(2):
        turn[...] = state_ref[k].reshape(128, 128).T
        for q in range(NL):
            for r in range(2):
                row = 128 * k + 16 * q + 8 * r
                st_ref[row : row + 8, :] = turn[pl.ds(2 * q + r, 8, stride=16), :]


def first_kernel(recv_ref, st_ref, out_ref, inv_ref, rhs_ref, fac_ref, scr):
    d = space()
    for s in range(ND):
        scr[s] = recv_ref[s, SRC1[0] : SRC1[0] + 32, :]

    @pl.when(is_last_slab())
    def _():
        edge = jnp.zeros((1, 128), F32)
        inv = [jnp.concatenate([edge, v, edge], axis=0) for v in inverse(recv_ref, 1, 11, d)]
        v = phi([recv_ref[s, TERM[0] : TERM[0] + 40, :] for s in range(ND)], inv)
        for s in range(ND):
            scr[s] = scr[s] + v[s][4:36]

    inv1 = inverse(recv_ref, 1, 4, d)
    rhs = phi([scr[s] for s in range(ND)], inverse(recv_ref, 0, 8, d))
    for s in range(ND):
        react0 = recv_ref[s, REACT + 1 : REACT + 2, :]
        inv_ref[s] = inv1[s]
        fac_ref[s] = 1.0 / (1.0 + 2.0 * (react0 + recv_ref[s, DAMP[0] + 11 : DAMP[0] + 27, :]))
        part = rhs[s][4:28] + recv_ref[s, SRC0[0] : SRC0[0] + 24, :]
        rhs_ref[s] = part[4:20]
        out_ref[41 * s : 41 * s + 24, :] = part
        out_ref[41 * s + 24 : 41 * s + 25, :] = react0
        out_ref[41 * s + 25 : 41 * s + 41, :] = st_ref[16 * s : 16 * s + 16, :]


def own_damp(recv1_ref):
    return recv1_ref[lax.axis_index("tl"), DAMP[0] + 7 : DAMP[0] + 31, :]


def compose_kernel(recv1_ref, recv_ref, out_ref):
    damp = own_damp(recv1_ref)
    carry = recv_ref[41 * (NL - 1) : 41 * (NL - 1) + 24, :]
    for j in range(NL - 2, -1, -1):
        react = recv_ref[41 * j + 24 : 41 * j + 25, :]
        carry = carry / (1.0 + 2.0 * (react + damp)) + recv_ref[41 * j : 41 * j + 24, :]
    group = lax.broadcasted_iota(jnp.int32, (1, 128), 1) // 16
    tail = recv_ref[24:25, :]
    for j in range(1, NL):
        tail = jnp.where(group == j, recv_ref[41 * j + 24 : 41 * j + 25, :], tail)
    for h in range(NH):
        out_ref[25 * h : 25 * h + 24, :] = carry
        out_ref[25 * h + 24 : 25 * h + 25, :] = tail


def scan_kernel(recv1_ref, recv2_ref, recv_ref, st_ref, out_ref):
    me = lax.axis_index("th")
    damp = own_damp(recv1_ref)
    carry = jnp.zeros((24, 128), F32)
    own_lanes = lax.broadcasted_iota(jnp.int32, (8, 128), 1) // 16 == lax.broadcasted_iota(jnp.int32, (8, 128), 0)
    for h in range(NH - 1, 0, -1):
        react = jnp.where(own_lanes, recv_ref[25 * h + 24 : 25 * h + 25, :], jnp.zeros((8, 128), F32))
        for shift in (16, 32, 64):
            react = react + pltpu.roll(react, shift, 1)
        den = None
        for j in range(NL):
            term = 1.0 + 2.0 * (react[j : j + 1] + damp)
            den = term if den is None else den * term
        carry = jnp.where(h > me, carry / den + recv_ref[25 * h : 25 * h + 24, :], carry)
    for j in range(NL - 1, -1, -1):
        out_ref[40 * j : 40 * j + 24, :] = carry
        out_ref[40 * j + 24 : 40 * j + 40, :] = st_ref[128 + 16 * j : 144 + 16 * j, :]
        react = recv2_ref[41 * j + 24 : 41 * j + 25, :]
        carry = carry / (1.0 + 2.0 * (react + damp)) + recv2_ref[41 * j : 41 * j + 24, :]


def final_kernel(recv1_ref, inv_ref, rhs_ref, fac_ref, recv_ref, out_ref, layers):
    last = is_last_slab()
    field = []
    for s in range(ND):
        incoming = recv_ref[40 * s : 40 * s + 24, :]
        layers[0, 16 * s : 16 * s + 16, :] = fac_ref[s] * incoming[4:20] + rhs_ref[s]
        field.append(jnp.where(last, recv1_ref[s, TERM[0] + 8 : TERM[0] + 32, :], incoming))
    w = phi(field, [inv_ref[s] for s in range(ND)])
    for s in range(ND):
        layers[1, 16 * s : 16 * s + 16, :] = w[s][4:20] + recv1_ref[s, SRC1[0] + 8 : SRC1[0] + 24, :]
    for s in range(ND):
        for k in range(2):
            for r in range(2):
                out_ref[pl.ds(4 * s + 2 * k + r, 8, stride=32), :] = layers[k, pl.ds(16 * s + r, 8, stride=2), :]


def product_kernel(recv2_ref, recv3_ref, recv_ref, out_ref):
    for r in range(2):
        total = jnp.zeros((8, 128), F32)
        for j in range(NL):
            first, second = 41 * j + 25 + 8 * r, 40 * j + 24 + 8 * r
            total = total + recv_ref[pl.ds(32 * j + r, 8, stride=4), :] * recv2_ref[first : first + 8, :]
            total = total + recv_ref[pl.ds(32 * j + 2 + r, 8, stride=4), :] * recv3_ref[second : second + 8, :]
        for h in range(NH):
            out_ref[16 * h + 8 * r : 16 * h + 8 * r + 8, :] = -total


def join_kernel(layers_ref, recv_ref, out_ref):
    total = recv_ref[0:16, :]
    for h in range(1, NH):
        total = total + recv_ref[16 * h : 16 * h + 16, :]
    for j in range(NL):
        out_ref[48 * j : 48 * j + 32, :] = layers_ref[32 * j : 32 * j + 32, :]
        out_ref[48 * j + 32 : 48 * j + 48, :] = total


def unpack_kernel(recv_ref, adj_ref, grad_ref, scr):
    for q in range(NL):
        for r in range(2):
            rows = pl.ds(2 * q + r, 8, stride=16)
            for k in range(2):
                scr[k, rows, :] = recv_ref[pl.ds(48 * q + 2 * k + r, 8, stride=4), :]
            scr[2, rows, :] = recv_ref[48 * q + 32 + 8 * r : 48 * q + 40 + 8 * r, :]
    for k in range(2):
        adj_ref[k] = scr[k].T.reshape(8, 16, 128)
    grad_ref[...] = scr[2].T.reshape(8, 16, 128)


VM = pl.BlockSpec(memory_space=pltpu.VMEM)
SM = pl.BlockSpec(memory_space=pltpu.SMEM)
INTERPRET = False


def near(value):
    return pltpu.with_memory_space_constraint(value, pltpu.VMEM)


def call(kernel, outs, in_specs, scratch=(), name=None):
    shapes = [jax.ShapeDtypeStruct(s[1:], F32) if s[0] is None else pltpu.VMEM(s, F32) for s in outs]
    single = len(shapes) == 1
    return pl.pallas_call(
        kernel,
        out_shape=shapes[0] if single else shapes,
        in_specs=in_specs,
        out_specs=VM if single else [VM] * len(shapes),
        scratch_shapes=list(scratch),
        name=name,
        interpret=INTERPRET,
    )


def shards(sources, forward_states, terminal, damping, contact_stiff, regions):
    def exchange(v, axes, slots=8):
        rows = v.size // (128 * slots)
        whole = rows % 8 == 0 or rows == 4
        v3 = v.reshape(slots, rows, 128) if whole else v.reshape(slots, 1, rows * 128)
        return near(lax.all_to_all(v3, axes, 0, 0, tiled=True).reshape(v.shape))

    def scratch(rows):
        return pltpu.VMEM((rows, 128), F32)

    xy, group = ("sx", "sy"), ("tl", "sx", "sy")
    send1, pieces = call(
        pack_kernel, [(ND, ROWS1, 128), (256, 128)], [SM, SM] + [VM] * 4, [scratch(152), scratch(128)], "pack"
    )(contact_stiff, regions, sources, damping, terminal, forward_states)
    pieces = near(pieces)
    recv1 = exchange(send1, xy)
    send2, inv1, rhs, fac = call(
        first_kernel,
        [(328, 128), (8, 24, 128), (8, 16, 128), (8, 16, 128)],
        [VM, VM],
        [pltpu.VMEM((8, 32, 128), F32)],
        "first",
    )(recv1, pieces)
    recv2 = exchange(send2, "tl")
    send_h = call(compose_kernel, [(200, 128)], [VM, VM], name="compose")(recv1, recv2)
    recv_h = exchange(send_h, "th")
    send3 = call(scan_kernel, [(320, 128)], [VM] * 4, name="scan")(recv1, recv2, recv_h, pieces)
    recv3 = exchange(send3, "tl")
    layers = call(final_kernel, [(256, 128)], [VM] * 5, [pltpu.VMEM((2, 128, 128), F32)], "final")(
        recv1, near(inv1), near(rhs), near(fac), recv3
    )
    layers = exchange(layers, group, 64)
    part = call(product_kernel, [(128, 128)], [VM] * 3, name="product")(recv2, recv3, layers)
    part = exchange(part, "th")
    joined = call(join_kernel, [(384, 128)], [VM, VM], name="join")(layers, part)
    joined = exchange(joined, "tl")
    return tuple(
        call(
            unpack_kernel,
            [(None, 2, 8, 16, 128), (None, 8, 16, 128)],
            [VM],
            [pltpu.VMEM((3, 128, 128), F32)],
            "unpack",
        )(joined)
    )


def solution(mesh):
    split = Mesh(mesh.devices.reshape(NH, NL, 4, 2), ("th", "tl", "sx", "sy"))
    tm = ("th", "tl")
    in_specs = (
        P(tm, "sx", "sy", None),
        P(tm, "sx", "sy", None),
        P("sx", "sy", None),
        P("sx", "sy", None),
        P(),
        P(tm, "sx", "sy"),
    )
    out_specs = (P(tm, "sx", "sy", None), P("sx", "sy", None))
    return jax.shard_map(shards, mesh=split, in_specs=in_specs, out_specs=out_specs, check_vma=False)
```

```python
import jax
import jax.numpy as jnp
from jax import lax
from jax.experimental import pallas as pl
from jax.experimental.pallas import tpu as pltpu
from jax.sharding import Mesh
from jax.sharding import PartitionSpec as P

F32 = jnp.float32
COUPLING = 0.5
CENTRE = 1.0 + 6.0 * COUPLING

NH, NL, ND = 8, 8, 8

T_OWN = 16
SRC1 = (0, 32, 8)
TERM = (32, 40, 12)
SRC0 = (72, 24, 4)
DAMP = (96, 38, 11)
REACT = 134
ROWS1 = 136


def neighbours(field):
    rows = field[0].shape[0]
    zero = jnp.zeros_like(field[0])
    lane = lax.broadcasted_iota(jnp.int32, field[0].shape, 1)
    yl = lane % 16
    after = [pltpu.roll(f, 112, 1) for f in field] + [zero, zero]
    before = [zero, zero] + [pltpu.roll(f, 16, 1) for f in field]
    out = []
    for s, f in enumerate(field):
        total = pltpu.roll(f, 1, 0) + pltpu.roll(f, rows - 1, 0)
        total = total + jnp.where(lane < 112, after[s], after[s + 2])
        total = total + jnp.where(lane >= 16, before[s + 2], before[s])
        other = pltpu.roll(field[s ^ 1], 15 if s % 2 == 0 else 113, 1)
        total = total + jnp.where(yl < 15, pltpu.roll(f, 127, 1), other if s % 2 == 0 else zero)
        total = total + jnp.where(yl > 0, pltpu.roll(f, 1, 1), zero if s % 2 == 0 else other)
        out.append(total)
    return out


def phi(b, inv):
    x = b
    for _ in range(4):
        x = [(b[s] + COUPLING * n) * inv[s] for s, n in enumerate(neighbours(x))]
    return x


def row_mask(rows, halo, d):
    t = lax.broadcasted_iota(jnp.int32, (rows, 128), 0) + d * T_OWN - halo
    return (t >= 0) & (t < 128)


def inverse(recv_ref, step, halo, d):
    rows = T_OWN + 2 * halo
    first = DAMP[0] + DAMP[2] - halo
    inside = row_mask(rows, halo, d)
    out = []
    for s in range(ND):
        react = recv_ref[s, REACT + 1 - step : REACT + 2 - step, :]
        diag = CENTRE + (react + recv_ref[s, first : first + rows, :])
        out.append(jnp.where(inside, 1.0 / diag, jnp.zeros_like(diag)))
    return out


def is_last_slab():
    return (lax.axis_index("th") == NH - 1) & (lax.axis_index("tl") == NL - 1)


def space():
    return lax.axis_index("sx") * 2 + lax.axis_index("sy")


def pack_kernel(stiff_ref, reg_ref, src_ref, damp_ref, term_ref, state_ref, out_ref, st_ref, pad, turn):
    def put(value, spec):
        off, rows, halo = spec
        pad[halo : halo + 128, :] = value.reshape(128, 128).T
        pad[halo + 128 : 2 * halo + 128, :] = jnp.zeros((halo, 128), F32)
        pad[0:halo, :] = jnp.zeros((halo, 128), F32)
        for d in range(ND):
            out_ref[d, off : off + rows, :] = pad[T_OWN * d : T_OWN * d + rows, :]

    put(src_ref[1], SRC1)
    put(damp_ref[...], DAMP)
    put(term_ref[...], TERM)
    put(src_ref[0], SRC0)
    yl = lax.broadcasted_iota(jnp.int32, (2, 128), 1) % 16
    row = lax.broadcasted_iota(jnp.int32, (2, 128), 0)
    react = []
    for k in range(2):
        react.append(jnp.where(yl < 8, stiff_ref[reg_ref[k, 0, 0]], stiff_ref[reg_ref[k, 0, 1]]))
    tail = jnp.where(row == 0, react[1], react[0])
    for d in range(ND):
        out_ref[d, REACT : REACT + 2, :] = tail
    for k in range(2):
        turn[...] = state_ref[k].reshape(128, 128).T
        for q in range(NL):
            for r in range(2):
                st_ref[pl.ds(32 * q + 2 * k + r, 8, stride=4), :] = turn[pl.ds(2 * q + r, 8, stride=16), :]


def first_kernel(recv_ref, st_ref, out_ref, rhs_ref, scr):
    d = space()
    for s in range(ND):
        scr[s] = recv_ref[s, SRC1[0] : SRC1[0] + 32, :]

    @pl.when(is_last_slab())
    def _():
        edge = jnp.zeros((1, 128), F32)
        inv = [jnp.concatenate([edge, v, edge], axis=0) for v in inverse(recv_ref, 1, 11, d)]
        v = phi([recv_ref[s, TERM[0] : TERM[0] + 40, :] for s in range(ND)], inv)
        for s in range(ND):
            scr[s] = scr[s] + v[s][4:36]

    rhs = phi([scr[s] for s in range(ND)], inverse(recv_ref, 0, 8, d))
    for s in range(ND):
        react0 = recv_ref[s, REACT + 1 : REACT + 2, :]
        part = rhs[s][4:28] + recv_ref[s, SRC0[0] : SRC0[0] + 24, :]
        rhs_ref[s] = part[4:20]
        out_ref[64 * s : 64 * s + 24, :] = part
        out_ref[64 * s + 24 : 64 * s + 32, :] = jnp.broadcast_to(react0, (8, 128))
        out_ref[64 * s + 32 : 64 * s + 64, :] = st_ref[32 * s : 32 * s + 32, :]


def own_damp(recv1_ref):
    return recv1_ref[lax.axis_index("tl"), DAMP[0] + 7 : DAMP[0] + 31, :]


def compose_kernel(recv1_ref, recv_ref, out_ref):
    damp = own_damp(recv1_ref)
    carry = recv_ref[64 * (NL - 1) : 64 * (NL - 1) + 24, :]
    for j in range(NL - 2, -1, -1):
        react = recv_ref[64 * j + 24 : 64 * j + 25, :]
        carry = carry / (1.0 + 2.0 * (react + damp)) + recv_ref[64 * j : 64 * j + 24, :]
    group = lax.broadcasted_iota(jnp.int32, (1, 128), 1) // 16
    tail = recv_ref[24:25, :]
    for j in range(1, NL):
        tail = jnp.where(group == j, recv_ref[64 * j + 24 : 64 * j + 25, :], tail)
    for h in range(NH):
        out_ref[25 * h : 25 * h + 24, :] = carry
        out_ref[25 * h + 24 : 25 * h + 25, :] = tail


def scan_kernel(recv1_ref, recv2_ref, recv_ref, out_ref):
    me = lax.axis_index("th")
    damp = own_damp(recv1_ref)
    carry = jnp.zeros((24, 128), F32)
    own_lanes = lax.broadcasted_iota(jnp.int32, (8, 128), 1) // 16 == lax.broadcasted_iota(jnp.int32, (8, 128), 0)
    for h in range(NH - 1, 0, -1):
        react = jnp.where(own_lanes, recv_ref[25 * h + 24 : 25 * h + 25, :], jnp.zeros((8, 128), F32))
        for shift in (16, 32, 64):
            react = react + pltpu.roll(react, shift, 1)
        den = None
        for j in range(NL):
            term = 1.0 + 2.0 * (react[j : j + 1] + damp)
            den = term if den is None else den * term
        carry = jnp.where(h > me, carry / den + recv_ref[25 * h : 25 * h + 24, :], carry)
    for j in range(NL - 1, -1, -1):
        out_ref[24 * j : 24 * j + 24, :] = carry
        react = recv2_ref[64 * j + 24 : 64 * j + 25, :]
        carry = carry / (1.0 + 2.0 * (react + damp)) + recv2_ref[64 * j : 64 * j + 24, :]


def final_kernel(recv1_ref, rhs_ref, recv_ref, out_ref, layers):
    last = is_last_slab()
    field = []
    for s in range(ND):
        incoming = recv_ref[24 * s : 24 * s + 24, :]
        react0 = recv1_ref[s, REACT + 1 : REACT + 2, :]
        factor = 1.0 / (1.0 + 2.0 * (react0 + recv1_ref[s, DAMP[0] + 11 : DAMP[0] + 27, :]))
        layers[0, 16 * s : 16 * s + 16, :] = factor * incoming[4:20] + rhs_ref[s]
        field.append(jnp.where(last, recv1_ref[s, TERM[0] + 8 : TERM[0] + 32, :], incoming))
    w = phi(field, inverse(recv1_ref, 1, 4, space()))
    for s in range(ND):
        layers[1, 16 * s : 16 * s + 16, :] = w[s][4:20] + recv1_ref[s, SRC1[0] + 8 : SRC1[0] + 24, :]
    for s in range(ND):
        for k in range(2):
            for r in range(2):
                out_ref[pl.ds(4 * s + 2 * k + r, 8, stride=32), :] = layers[k, pl.ds(16 * s + r, 8, stride=2), :]


def product_kernel(recv2_ref, recv_ref, out_ref, scr):
    total = recv_ref[0:32, :] * recv2_ref[32:64, :]
    for j in range(1, NL):
        total = total + recv_ref[32 * j : 32 * j + 32, :] * recv2_ref[64 * j + 32 : 64 * j + 64, :]
    scr[...] = -total
    for r in range(2):
        rows = scr[pl.ds(r, 8, stride=4), :] + scr[pl.ds(2 + r, 8, stride=4), :]
        for h in range(NH):
            out_ref[16 * h + 8 * r : 16 * h + 8 * r + 8, :] = rows


def join_kernel(layers_ref, recv_ref, out_ref):
    total = recv_ref[0:16, :]
    for h in range(1, NH):
        total = total + recv_ref[16 * h : 16 * h + 16, :]
    for j in range(NL):
        out_ref[48 * j : 48 * j + 32, :] = layers_ref[32 * j : 32 * j + 32, :]
        out_ref[48 * j + 32 : 48 * j + 48, :] = total


def unpack_kernel(recv_ref, adj_ref, grad_ref, scr):
    for q in range(NL):
        for r in range(2):
            rows = pl.ds(2 * q + r, 8, stride=16)
            for k in range(2):
                scr[k, rows, :] = recv_ref[pl.ds(48 * q + 2 * k + r, 8, stride=4), :]
            scr[2, rows, :] = recv_ref[48 * q + 32 + 8 * r : 48 * q + 40 + 8 * r, :]
    for k in range(2):
        adj_ref[k] = scr[k].T.reshape(8, 16, 128)
    grad_ref[...] = scr[2].T.reshape(8, 16, 128)


VM = pl.BlockSpec(memory_space=pltpu.VMEM)
SM = pl.BlockSpec(memory_space=pltpu.SMEM)
INTERPRET = False


def near(value):
    return pltpu.with_memory_space_constraint(value, pltpu.VMEM)


def call(kernel, outs, in_specs, scratch=(), name=None):
    shapes = [jax.ShapeDtypeStruct(s[1:], F32) if s[0] is None else pltpu.VMEM(s, F32) for s in outs]
    single = len(shapes) == 1
    return pl.pallas_call(
        kernel,
        out_shape=shapes[0] if single else shapes,
        in_specs=in_specs,
        out_specs=VM if single else [VM] * len(shapes),
        scratch_shapes=list(scratch),
        name=name,
        interpret=INTERPRET,
    )


def shards(sources, forward_states, terminal, damping, contact_stiff, regions):
    def exchange(v, axes, slots=8):
        rows = v.size // (128 * slots)
        whole = rows % 8 == 0 or rows == 4
        v3 = v.reshape(slots, rows, 128) if whole else v.reshape(slots, 1, rows * 128)
        return near(lax.all_to_all(v3, axes, 0, 0, tiled=True).reshape(v.shape))

    def scratch(rows):
        return pltpu.VMEM((rows, 128), F32)

    xy, group = ("sx", "sy"), ("tl", "sx", "sy")
    send1, pieces = call(
        pack_kernel, [(ND, ROWS1, 128), (256, 128)], [SM, SM] + [VM] * 4, [scratch(152), scratch(128)], "pack"
    )(contact_stiff, regions, sources, damping, terminal, forward_states)
    recv1 = exchange(send1, xy)
    send2, rhs = call(
        first_kernel,
        [(512, 128), (8, 16, 128)],
        [VM, VM],
        [pltpu.VMEM((8, 32, 128), F32)],
        "first",
    )(recv1, near(pieces))
    recv2 = exchange(send2, "tl")
    send_h = call(compose_kernel, [(200, 128)], [VM, VM], name="compose")(recv1, recv2)
    recv_h = exchange(send_h, "th")
    send3 = call(scan_kernel, [(192, 128)], [VM] * 3, name="scan")(recv1, recv2, recv_h)
    recv3 = exchange(send3, "tl")
    layers = call(final_kernel, [(256, 128)], [VM] * 3, [pltpu.VMEM((2, 128, 128), F32)], "final")(
        recv1, near(rhs), recv3
    )
    layers = exchange(layers, group, 64)
    part = call(product_kernel, [(128, 128)], [VM, VM], [scratch(32)], "product")(recv2, layers)
    part = exchange(part, "th")
    joined = call(join_kernel, [(384, 128)], [VM, VM], name="join")(layers, part)
    joined = exchange(joined, "tl")
    return tuple(
        call(
            unpack_kernel,
            [(None, 2, 8, 16, 128), (None, 8, 16, 128)],
            [VM],
            [pltpu.VMEM((3, 128, 128), F32)],
            "unpack",
        )(joined)
    )


def solution(mesh):
    split = Mesh(mesh.devices.reshape(NH, NL, 4, 2), ("th", "tl", "sx", "sy"))
    tm = ("th", "tl")
    in_specs = (
        P(tm, "sx", "sy", None),
        P(tm, "sx", "sy", None),
        P("sx", "sy", None),
        P("sx", "sy", None),
        P(),
        P(tm, "sx", "sy"),
    )
    out_specs = (P(tm, "sx", "sy", None), P("sx", "sy", None))
    return jax.shard_map(shards, mesh=split, in_specs=in_specs, out_specs=out_specs, check_vma=False)
```

```python
import jax
import jax.numpy as jnp
from jax import lax
from jax.experimental import pallas as pl
from jax.experimental.pallas import tpu as pltpu
from jax.sharding import Mesh
from jax.sharding import PartitionSpec as P

F32 = jnp.float32
COUPLING = 0.5
CENTRE = 1.0 + 6.0 * COUPLING

NH, NL, ND = 8, 8, 8

T_OWN = 16
SRC1 = (0, 32, 8)
TERM = (32, 40, 12)
SRC0 = (72, 24, 4)
DAMP = (96, 38, 11)
REACT = 134
ROWS1 = 136


def neighbours(field):
    rows = field[0].shape[0]
    zero = jnp.zeros_like(field[0])
    lane = lax.broadcasted_iota(jnp.int32, field[0].shape, 1)
    yl = lane % 16
    after = [pltpu.roll(f, 112, 1) for f in field] + [zero, zero]
    before = [zero, zero] + [pltpu.roll(f, 16, 1) for f in field]
    out = []
    for s, f in enumerate(field):
        total = pltpu.roll(f, 1, 0) + pltpu.roll(f, rows - 1, 0)
        total = total + jnp.where(lane < 112, after[s], after[s + 2])
        total = total + jnp.where(lane >= 16, before[s + 2], before[s])
        other = pltpu.roll(field[s ^ 1], 15 if s % 2 == 0 else 113, 1)
        total = total + jnp.where(yl < 15, pltpu.roll(f, 127, 1), other if s % 2 == 0 else zero)
        total = total + jnp.where(yl > 0, pltpu.roll(f, 1, 1), zero if s % 2 == 0 else other)
        out.append(total)
    return out


def phi(b, inv):
    x = b
    for _ in range(4):
        x = [(b[s] + COUPLING * n) * inv[s] for s, n in enumerate(neighbours(x))]
    return x


def row_mask(rows, halo, d):
    t = lax.broadcasted_iota(jnp.int32, (rows, 128), 0) + d * T_OWN - halo
    return (t >= 0) & (t < 128)


def inverse(recv_ref, step, halo, d):
    rows = T_OWN + 2 * halo
    first = DAMP[0] + DAMP[2] - halo
    inside = row_mask(rows, halo, d)
    out = []
    for s in range(ND):
        react = recv_ref[s, REACT + 1 - step : REACT + 2 - step, :]
        diag = CENTRE + (react + recv_ref[s, first : first + rows, :])
        out.append(jnp.where(inside, 1.0 / diag, jnp.zeros_like(diag)))
    return out


def is_last_slab():
    return (lax.axis_index("th") == NH - 1) & (lax.axis_index("tl") == NL - 1)


def space():
    return lax.axis_index("sx") * 2 + lax.axis_index("sy")


def pack_kernel(stiff_ref, reg_ref, src_ref, damp_ref, term_ref, state_ref, out_ref, st_ref, pad, turn):
    def put(value, spec):
        off, rows, halo = spec
        pad[halo : halo + 128, :] = value.reshape(128, 128).T
        pad[halo + 128 : 2 * halo + 128, :] = jnp.zeros((halo, 128), F32)
        pad[0:halo, :] = jnp.zeros((halo, 128), F32)
        for d in range(ND):
            out_ref[d, off : off + rows, :] = pad[T_OWN * d : T_OWN * d + rows, :]

    put(src_ref[1], SRC1)
    put(damp_ref[...], DAMP)
    put(term_ref[...], TERM)
    put(src_ref[0], SRC0)
    yl = lax.broadcasted_iota(jnp.int32, (2, 128), 1) % 16
    row = lax.broadcasted_iota(jnp.int32, (2, 128), 0)
    react = []
    for k in range(2):
        react.append(jnp.where(yl < 8, stiff_ref[reg_ref[k, 0, 0]], stiff_ref[reg_ref[k, 0, 1]]))
    tail = jnp.where(row == 0, react[1], react[0])
    for d in range(ND):
        out_ref[d, REACT : REACT + 2, :] = tail
    for k in range(2):
        turn[...] = state_ref[k].reshape(128, 128).T
        for q in range(NL):
            for r in range(2):
                row = 128 * k + 16 * q + 8 * r
                st_ref[row : row + 8, :] = turn[pl.ds(2 * q + r, 8, stride=16), :]


def first_kernel(recv_ref, st_ref, out_ref, inv_ref, rhs_ref, fac_ref, scr):
    d = space()
    for s in range(ND):
        scr[s] = recv_ref[s, SRC1[0] : SRC1[0] + 32, :]

    @pl.when(is_last_slab())
    def _():
        edge = jnp.zeros((1, 128), F32)
        inv = [jnp.concatenate([edge, v, edge], axis=0) for v in inverse(recv_ref, 1, 11, d)]
        v = phi([recv_ref[s, TERM[0] : TERM[0] + 40, :] for s in range(ND)], inv)
        for s in range(ND):
            scr[s] = scr[s] + v[s][4:36]

    inv1 = inverse(recv_ref, 1, 4, d)
    rhs = phi([scr[s] for s in range(ND)], inverse(recv_ref, 0, 8, d))
    for s in range(ND):
        react0 = recv_ref[s, REACT + 1 : REACT + 2, :]
        inv_ref[s] = inv1[s]
        fac_ref[s] = 1.0 / (1.0 + 2.0 * (react0 + recv_ref[s, DAMP[0] + 11 : DAMP[0] + 27, :]))
        part = rhs[s][4:28] + recv_ref[s, SRC0[0] : SRC0[0] + 24, :]
        rhs_ref[s] = part[4:20]
        out_ref[41 * s : 41 * s + 24, :] = part
        out_ref[41 * s + 24 : 41 * s + 25, :] = react0
        out_ref[41 * s + 25 : 41 * s + 41, :] = st_ref[16 * s : 16 * s + 16, :]


def own_damp(recv1_ref):
    return recv1_ref[lax.axis_index("tl"), DAMP[0] + 7 : DAMP[0] + 31, :]


def compose_kernel(recv1_ref, recv_ref, out_ref):
    damp = own_damp(recv1_ref)
    carry = recv_ref[41 * (NL - 1) : 41 * (NL - 1) + 24, :]
    for j in range(NL - 2, -1, -1):
        react = recv_ref[41 * j + 24 : 41 * j + 25, :]
        carry = carry * (1.0 / (1.0 + 2.0 * (react + damp))) + recv_ref[41 * j : 41 * j + 24, :]
    group = lax.broadcasted_iota(jnp.int32, (1, 128), 1) // 16
    tail = recv_ref[24:25, :]
    for j in range(1, NL):
        tail = jnp.where(group == j, recv_ref[41 * j + 24 : 41 * j + 25, :], tail)
    for h in range(NH):
        out_ref[25 * h : 25 * h + 24, :] = carry
        out_ref[25 * h + 24 : 25 * h + 25, :] = tail


def scan_kernel(recv1_ref, recv2_ref, recv_ref, st_ref, out_ref):
    me = lax.axis_index("th")
    damp = own_damp(recv1_ref)
    carry = jnp.zeros((24, 128), F32)
    own_lanes = lax.broadcasted_iota(jnp.int32, (8, 128), 1) // 16 == lax.broadcasted_iota(jnp.int32, (8, 128), 0)
    for h in range(NH - 1, 0, -1):
        react = jnp.where(own_lanes, recv_ref[25 * h + 24 : 25 * h + 25, :], jnp.zeros((8, 128), F32))
        for shift in (16, 32, 64):
            react = react + pltpu.roll(react, shift, 1)
        den = None
        for j in range(NL):
            term = 1.0 + 2.0 * (react[j : j + 1] + damp)
            den = term if den is None else den * term
        carry = jnp.where(h > me, carry * (1.0 / den) + recv_ref[25 * h : 25 * h + 24, :], carry)
    for j in range(NL - 1, -1, -1):
        out_ref[40 * j : 40 * j + 24, :] = carry
        out_ref[40 * j + 24 : 40 * j + 40, :] = st_ref[128 + 16 * j : 144 + 16 * j, :]
        react = recv2_ref[41 * j + 24 : 41 * j + 25, :]
        carry = carry * (1.0 / (1.0 + 2.0 * (react + damp))) + recv2_ref[41 * j : 41 * j + 24, :]


def final_kernel(recv1_ref, inv_ref, rhs_ref, fac_ref, recv_ref, out_ref, layers):
    last = is_last_slab()
    field = []
    for s in range(ND):
        incoming = recv_ref[40 * s : 40 * s + 24, :]
        layers[0, 16 * s : 16 * s + 16, :] = fac_ref[s] * incoming[4:20] + rhs_ref[s]
        field.append(jnp.where(last, recv1_ref[s, TERM[0] + 8 : TERM[0] + 32, :], incoming))
    w = phi(field, [inv_ref[s] for s in range(ND)])
    for s in range(ND):
        layers[1, 16 * s : 16 * s + 16, :] = w[s][4:20] + recv1_ref[s, SRC1[0] + 8 : SRC1[0] + 24, :]
    for s in range(ND):
        for k in range(2):
            for r in range(2):
                out_ref[pl.ds(4 * s + 2 * k + r, 8, stride=32), :] = layers[k, pl.ds(16 * s + r, 8, stride=2), :]


def product_kernel(recv2_ref, recv3_ref, recv_ref, out_ref):
    for r in range(2):
        total = jnp.zeros((8, 128), F32)
        for j in range(NL):
            first, second = 41 * j + 25 + 8 * r, 40 * j + 24 + 8 * r
            total = total + recv_ref[pl.ds(32 * j + r, 8, stride=4), :] * recv2_ref[first : first + 8, :]
            total = total + recv_ref[pl.ds(32 * j + 2 + r, 8, stride=4), :] * recv3_ref[second : second + 8, :]
        for h in range(NH):
            out_ref[16 * h + 8 * r : 16 * h + 8 * r + 8, :] = -total


def join_kernel(layers_ref, recv_ref, out_ref):
    total = recv_ref[0:16, :]
    for h in range(1, NH):
        total = total + recv_ref[16 * h : 16 * h + 16, :]
    for j in range(NL):
        out_ref[48 * j : 48 * j + 32, :] = layers_ref[32 * j : 32 * j + 32, :]
        out_ref[48 * j + 32 : 48 * j + 48, :] = total


def unpack_kernel(recv_ref, adj_ref, grad_ref, scr):
    for q in range(NL):
        for r in range(2):
            rows = pl.ds(2 * q + r, 8, stride=16)
            for k in range(2):
                scr[k, rows, :] = recv_ref[pl.ds(48 * q + 2 * k + r, 8, stride=4), :]
            scr[2, rows, :] = recv_ref[48 * q + 32 + 8 * r : 48 * q + 40 + 8 * r, :]
    for k in range(2):
        adj_ref[k] = scr[k].T.reshape(8, 16, 128)
    grad_ref[...] = scr[2].T.reshape(8, 16, 128)


VM = pl.BlockSpec(memory_space=pltpu.VMEM)
SM = pl.BlockSpec(memory_space=pltpu.SMEM)
INTERPRET = False


def near(value):
    return pltpu.with_memory_space_constraint(value, pltpu.VMEM)


def call(kernel, outs, in_specs, scratch=(), name=None):
    shapes = [jax.ShapeDtypeStruct(s[1:], F32) if s[0] is None else pltpu.VMEM(s, F32) for s in outs]
    single = len(shapes) == 1
    return pl.pallas_call(
        kernel,
        out_shape=shapes[0] if single else shapes,
        in_specs=in_specs,
        out_specs=VM if single else [VM] * len(shapes),
        scratch_shapes=list(scratch),
        name=name,
        interpret=INTERPRET,
    )


def shards(sources, forward_states, terminal, damping, contact_stiff, regions):
    def exchange(v, axes, slots=8):
        rows = v.size // (128 * slots)
        whole = rows % 8 == 0 or rows == 4
        v3 = v.reshape(slots, rows, 128) if whole else v.reshape(slots, 1, rows * 128)
        return near(lax.all_to_all(v3, axes, 0, 0, tiled=True).reshape(v.shape))

    def scratch(rows):
        return pltpu.VMEM((rows, 128), F32)

    xy, group = ("sx", "sy"), ("tl", "sx", "sy")
    send1, pieces = call(
        pack_kernel, [(ND, ROWS1, 128), (256, 128)], [SM, SM] + [VM] * 4, [scratch(152), scratch(128)], "pack"
    )(contact_stiff, regions, sources, damping, terminal, forward_states)
    pieces = near(pieces)
    recv1 = exchange(send1, xy)
    send2, inv1, rhs, fac = call(
        first_kernel,
        [(328, 128), (8, 24, 128), (8, 16, 128), (8, 16, 128)],
        [VM, VM],
        [pltpu.VMEM((8, 32, 128), F32)],
        "first",
    )(recv1, pieces)
    recv2 = exchange(send2, "tl")
    send_h = call(compose_kernel, [(200, 128)], [VM, VM], name="compose")(recv1, recv2)
    recv_h = exchange(send_h, "th")
    send3 = call(scan_kernel, [(320, 128)], [VM] * 4, name="scan")(recv1, recv2, recv_h, pieces)
    recv3 = exchange(send3, "tl")
    layers = call(final_kernel, [(256, 128)], [VM] * 5, [pltpu.VMEM((2, 128, 128), F32)], "final")(
        recv1, near(inv1), near(rhs), near(fac), recv3
    )
    layers = exchange(layers, group, 64)
    part = call(product_kernel, [(128, 128)], [VM] * 3, name="product")(recv2, recv3, layers)
    part = exchange(part, "th")
    joined = call(join_kernel, [(384, 128)], [VM, VM], name="join")(layers, part)
    joined = exchange(joined, "tl")
    return tuple(
        call(
            unpack_kernel,
            [(None, 2, 8, 16, 128), (None, 8, 16, 128)],
            [VM],
            [pltpu.VMEM((3, 128, 128), F32)],
            "unpack",
        )(joined)
    )


def solution(mesh):
    split = Mesh(mesh.devices.reshape(NH, NL, 4, 2), ("th", "tl", "sx", "sy"))
    tm = ("th", "tl")
    in_specs = (
        P(tm, "sx", "sy", None),
        P(tm, "sx", "sy", None),
        P("sx", "sy", None),
        P("sx", "sy", None),
        P(),
        P(tm, "sx", "sy"),
    )
    out_specs = (P(tm, "sx", "sy", None), P("sx", "sy", None))
    return jax.shard_map(shards, mesh=split, in_specs=in_specs, out_specs=out_specs, check_vma=False)
```
